32 devices in a mesh: dp: 2 (over core), blk: 4 (over z), uly: 4 (over y, x).
Axes of the slice: x: 2, y: 2, z: 4, core: 2. Of those that a mesh axis runs over, the one named last changes fastest.
Arguments:
- tokens: bfloat16 [4, 1024, 1536], P('dp', ('blk', 'uly')), may hold values from -6 to 6
- cotangent: bfloat16 [4, 1024, 1536], P('dp', ('blk', 'uly')), may hold values from -6 to 6
- lengths: int32 [4], P('dp'), may hold values from 256 to 1024, as said below
- owner_slot: int32 [2856], replicated, may hold values from 0 to 2879, as said below
- master: float32 [2880, 128, 128], P(('dp', 'blk', 'uly'))
- moment_first: float32 [2880, 128, 128], P(('dp', 'blk', 'uly'))
- moment_second: float32 [2880, 128, 128], P(('dp', 'blk', 'uly')), as said below
- basis_left: float32 [2880, 128, 128], P(('dp', 'blk', 'uly')), as said below
- basis_right: float32 [2880, 128, 128], P(('dp', 'blk', 'uly')), as said below
- small_master: float32 [5120], P(('dp', 'blk', 'uly'))
- small_first: float32 [5120], P(('dp', 'blk', 'uly')), may hold values from -181.01933 to 181.01933
- small_second: float32 [5120], P(('dp', 'blk', 'uly')), may hold values from 2048 to 8192
Outputs:
- mixed: bfloat16 [4, 1024, 1536], P('dp', ('blk', 'uly'))
- grad_tokens: float32 [4, 1024, 1536], P('dp', ('blk', 'uly'))
- moment_first_new: float32 [2880, 128, 128], P(('dp', 'blk', 'uly'))
- moment_second_new: float32 [2880, 128, 128], P(('dp', 'blk', 'uly'))
- master_new: float32 [2880, 128, 128], P(('dp', 'blk', 'uly'))
- small_first_new: float32 [5120], P(('dp', 'blk', 'uly'))
- small_second_new: float32 [5120], P(('dp', 'blk', 'uly'))
- small_new: float32 [5120], P(('dp', 'blk', 'uly'))
The draws below stay inside these ranges and needn't reach their ends.
Inputs may be any that keep to these rules, and one draw needn't show every extreme that they name: `lengths`: at least 256 real tokens each, the rest padding; in every draw some sequence has all 1024. `owner_slot`: distinct slots; slot s is slot s % 90 of the device at position s // 90 in the order dp, blk, uly; the last slot is always used. `basis_left`: each slot's matrix is orthogonal. `basis_right`: each slot's matrix is orthogonal. `moment_second`: positive.
All inputs are finite; a program needn't handle non-finite values.
Results may differ from the reference program's by a relative error of at most 0.017.
Values may be sent and summed in bfloat16 or wider, within the bound.
No kernel may reach another device: no remote copies, remote signals or barrier semaphores. Data moves between devices by JAX's collectives and lax.ppermute only.
A program may use at most 704 MiB of HBM per device.

```python
import math
import jax
import jax.numpy as jnp
import numpy as np
from jax import lax

D = 1536
QH = 12
KVH = 2
HD = 128
FF = 8960
BLOCK = 128
QW = 1536
KVW = 256
LEN = 1024
SEQS = 4
SMALL = 5120
N_TILES = 2856
SLOTS = 2880


def matrix_shapes_drawn():
    return [(D, QW), (D, KVW), (D, KVW), (QW, D), (D, FF), (D, FF), (FF, D)]


def tile_kinds():
    kinds = []
    for number, shape_pair in enumerate(matrix_shapes_drawn()):
        kinds.append(np.full(shape_pair[0] // BLOCK * (shape_pair[1] // BLOCK), number, dtype=np.int32))
    return np.concatenate(kinds)


def owner_table(key):
    spare = jax.random.permutation(jax.random.fold_in(key, 11), SLOTS - 1)
    flags = jnp.zeros((SLOTS,), jnp.int32).at[spare[:SLOTS - N_TILES]].set(1)
    used_slots = jnp.argsort(flags, stable=True)[:N_TILES]
    shuffle = jax.random.permutation(jax.random.fold_in(key, 12), N_TILES)
    return used_slots[shuffle].astype(jnp.int32)


def slot_kinds(key):
    owners = owner_table(key)
    return jnp.full((SLOTS,), 7, jnp.int32).at[owners].set(jnp.asarray(tile_kinds()))


def grad_scales():
    base_scale = math.sqrt(0.5 * SEQS * LEN)
    return jnp.asarray([base_scale, base_scale, base_scale * math.sqrt(10.0 / LEN), base_scale, 0.6 * base_scale, 0.6 * base_scale, 0.6 * base_scale, base_scale], jnp.float32)


def weight_scales():
    return jnp.asarray([D ** (-0.5), D ** (-0.5), math.sqrt(LEN / (10.0 * D)), QW ** (-0.5), D ** (-0.5), D ** (-0.5), FF ** (-0.5), D ** (-0.5)], jnp.float32)


def signed_values(key, shape):
    return jax.random.truncated_normal(key, -4.0, 4.0, shape, jnp.float32)


def orthogonal_set(key):
    steps_row = jnp.arange(BLOCK, dtype=jnp.float32)
    table = jnp.sqrt(2.0 / BLOCK) * jnp.cos(math.pi * (2.0 * steps_row[:, None] + 1.0) * steps_row[None, :] / (2.0 * BLOCK))
    table = jnp.where(steps_row[None, :] == 0.0, math.sqrt(1.0 / BLOCK), table)
    orders = jax.vmap(lambda single: jax.random.permutation(single, BLOCK))(jax.random.split(jax.random.fold_in(key, 1), SLOTS))
    signs = (2 * jax.random.randint(jax.random.fold_in(key, 2), (SLOTS, BLOCK), 0, 2) - 1).astype(jnp.float32)
    return signs[:, :, None] * jnp.take(table, orders, axis=1).transpose(1, 0, 2)


def draw_owner_slot(key, part):
    return owner_table(key)


def draw_lengths(key, part):
    drawn = jax.random.randint(jax.random.fold_in(key, 41), (SEQS,), LEN // 4, LEN + 1)
    longest = jax.random.randint(jax.random.fold_in(key, 42), (), 0, SEQS)
    return jnp.where(jnp.arange(SEQS) == longest, LEN, drawn).astype(jnp.int32)


def draw_master(key, part):
    kinds = slot_kinds(key)
    scales = jnp.take(weight_scales(), kinds)
    return signed_values(jax.random.fold_in(key, 21), (SLOTS, BLOCK, BLOCK)) * scales[:, None, None]


def draw_moment_first(key, part):
    kinds = slot_kinds(key)
    scales = jnp.take(grad_scales(), kinds)
    return signed_values(jax.random.fold_in(key, 22), (SLOTS, BLOCK, BLOCK)) * scales[:, None, None]


def draw_moment_second(key, part):
    kinds = slot_kinds(key)
    scales = jnp.take(grad_scales(), kinds)
    factor = jnp.exp(jax.random.uniform(jax.random.fold_in(key, 23), (SLOTS, BLOCK, BLOCK), jnp.float32, 0.0, math.log(4.0)))
    return factor * (scales * scales)[:, None, None]


def draw_basis_left(key, part):
    return orthogonal_set(jax.random.fold_in(key, 31))


def draw_basis_right(key, part):
    return orthogonal_set(jax.random.fold_in(key, 32))


def draw_small_master(key, part):
    gains = jax.random.uniform(jax.random.fold_in(key, 51), (2 * D,), jnp.float32, 0.7, 1.3)
    biases = 0.3 * jax.random.normal(jax.random.fold_in(key, 52), (QW + KVW,), jnp.float32)
    value_bias = 0.3 * jax.random.normal(jax.random.fold_in(key, 53), (KVW,), jnp.float32)
    return jnp.concatenate([gains, biases, value_bias])


def block_levels(key, shape, shards, low, top_value):
    def one(position, blocks):
        draws = jax.random.uniform(jax.random.fold_in(jax.random.fold_in(key, 6), position), (blocks,), jnp.float32, low / len(shards), top_value / len(shards))
        return jnp.repeat(jnp.exp(draws), shape[position] // blocks).reshape((-1,) + (1,) * (len(shape) - position - 1))

    factor_of = one(*shards[0])
    for cut in shards[1:]:
        factor_of = factor_of * one(*cut)
    return factor_of


def noise(key, shape, deviation, most, cuts=(), kind=jnp.bfloat16):
    entries = deviation * jax.random.normal(key, shape, jnp.float32)
    if cuts:
        entries = entries * block_levels(key, shape, cuts, -0.22, 0.18)
    return jnp.clip(entries, -most, most).astype(kind)


def setup_inputs(seed: int = 0) -> dict:
    streams_of = jax.random.split(jax.random.key(seed), 13)
    tokens = noise(streams_of[0], (SEQS, LEN, D), 1.0, 6.0, ((0, 2), (1, 16)))
    cotangent = noise(streams_of[1], (SEQS, LEN, D), 1.0, 6.0, ((0, 2), (1, 16)))
    lengths = draw_lengths(jax.random.fold_in(streams_of[12], 71), 0)
    owner_slot = draw_owner_slot(jax.random.fold_in(streams_of[12], 71), 0)
    master = draw_master(jax.random.fold_in(streams_of[12], 71), 0)
    moment_first = draw_moment_first(jax.random.fold_in(streams_of[12], 71), 0)
    moment_second = draw_moment_second(jax.random.fold_in(streams_of[12], 71), 0)
    basis_left = draw_basis_left(jax.random.fold_in(streams_of[12], 71), 0)
    basis_right = draw_basis_right(jax.random.fold_in(streams_of[12], 71), 0)
    small_master = draw_small_master(jax.random.fold_in(streams_of[12], 71), 0)
    small_first = noise(streams_of[10], (SMALL,), ((SEQS * LEN // 2) ** 0.5), 181.01933, ((0, 32),), jnp.float32)
    small_second = jnp.clip(jnp.exp(math.log(8192.0) - 1.3862944 * jax.random.uniform(streams_of[11], (SMALL,), jnp.float32) ** block_levels(streams_of[11], (SMALL,), ((0, 32),), -0.2, 0.2)), 2048.0, 8192.0)
    return dict(tokens=tokens, cotangent=cotangent, lengths=lengths, owner_slot=owner_slot, master=master, moment_first=moment_first, moment_second=moment_second, basis_left=basis_left, basis_right=basis_right, small_master=small_master, small_first=small_first, small_second=small_second)


@jax.custom_vjp
def low(v):
    return lax.optimization_barrier(v.astype(jnp.bfloat16)).astype(jnp.float32)

@jax.custom_vjp
def low_back(v):
    return v

def low_keep(v):
    return (low(v), None)

def low_pass(kept, grad):
    return (grad,)

def back_keep(v):
    return (v, None)

def back_low(kept, grad):
    return (low(grad),)
low.defvjp(low_keep, low_pass)
low_back.defvjp(back_keep, back_low)
NORM_EPS = 1e-06
ROPE_BASE = 1000000.0
BETA_FIRST = 0.5
BETA_SECOND = 0.5
ADAM_EPS = 1e-08
SCALE_EPS = 1e-06
RELATIVE_RATE = 0.5
SMALL_RATE = 0.25
WEIGHT_DECAY = 0.01
MASK_FILL = -1e+30
TOP_PRECISION = lax.Precision.HIGHEST

def matrix_shapes():
    return [(D, QW), (D, KVW), (D, KVW), (QW, D), (D, FF), (D, FF), (FF, D)]

def assemble(tile_set):
    matrices = []
    offset = 0
    for row_count, col_count in matrix_shapes():
        tile_count = row_count // BLOCK * (col_count // BLOCK)
        blocked = tile_set[offset:offset + tile_count].reshape(row_count // BLOCK, col_count // BLOCK, BLOCK, BLOCK)
        matrices.append(blocked.transpose(0, 2, 1, 3).reshape(row_count, col_count))
        offset = offset + tile_count
    return matrices

def disassemble(matrices):
    pieces = []
    for matrix in matrices:
        row_count, col_count = matrix.shape
        blocked = matrix.reshape(row_count // BLOCK, BLOCK, col_count // BLOCK, BLOCK).transpose(0, 2, 1, 3)
        pieces.append(blocked.reshape(-1, BLOCK, BLOCK))
    return jnp.concatenate(pieces, axis=0)

def split_small(vector):
    edges = [0, D, 2 * D, 2 * D + QW, 2 * D + QW + KVW, 2 * D + QW + 2 * KVW]
    return [vector[edges[number]:edges[number + 1]] for number in range(5)]

def rms_norm(values, gain):
    inverse = lax.rsqrt(lax.optimization_barrier(jnp.mean(values * values, axis=-1, keepdims=True)) + NORM_EPS)
    return values * inverse * gain

def rotate(values, positions, direction):
    half_size = HD // 2
    frequency = ROPE_BASE ** (-2.0 * jnp.arange(half_size, dtype=jnp.float32) / HD)
    angles = positions.astype(jnp.float32)[:, None] * frequency[None, :]
    cosine = jnp.cos(angles)[:, None, :]
    sine = direction * jnp.sin(angles)[:, None, :]
    first_half = values[..., :half_size]
    second_half = values[..., half_size:]
    return jnp.concatenate([first_half * cosine - second_half * sine, second_half * cosine + first_half * sine], axis=-1)

def product(left_side, right_side):
    return jnp.dot(left_side, right_side, precision=TOP_PRECISION, preferred_element_type=jnp.float32)

def layer_sequence(params, values, length):
    w_query, w_key, w_value, w_out, w_gate, w_up, w_down, gain_first, gain_second, bias_query, bias_key, bias_value = params
    positions = jnp.arange(LEN, dtype=jnp.int32)
    normed = low(rms_norm(values, gain_first))
    query_lin = low_back(product(normed, w_query) + bias_query)
    key_lin = low_back(product(normed, w_key) + bias_key)
    value_low = low(low_back(product(normed, w_value) + bias_value))
    query_rot = low(low_back(rotate(query_lin.reshape(LEN, QH, HD), positions, 1.0)))
    key_rot = low(low_back(rotate(key_lin.reshape(LEN, KVH, HD), positions, 1.0)))
    keys_wide = jnp.repeat(key_rot, QH // KVH, axis=1)
    values_wide = jnp.repeat(value_low.reshape(LEN, KVH, HD), QH // KVH, axis=1)
    block_rows = math.gcd(LEN, 512)

    def attend(inputs):
        query_block, first_row = inputs
        scores = jnp.einsum('qhd,khd->hqk', query_block, keys_wide, precision=TOP_PRECISION) / math.sqrt(HD)
        scores = low_back(scores)
        query_pos = first_row + jnp.arange(block_rows, dtype=jnp.int32)
        allowed = (positions[None, :] <= query_pos[:, None]) & (positions[None, :] < length)
        probs = jax.nn.softmax(jnp.where(allowed[None], scores, MASK_FILL), axis=-1)
        return jnp.einsum('hqk,khd->qhd', probs, values_wide, precision=TOP_PRECISION)
    first_rows = jnp.arange(LEN // block_rows, dtype=jnp.int32) * block_rows
    attended = lax.map(jax.checkpoint(attend), (query_rot.reshape(LEN // block_rows, block_rows, QH, HD), first_rows))
    attended_low = low(low_back(attended.reshape(LEN, QW)))
    middle = values + low_back(product(attended_low, w_out))
    normed_two = low(rms_norm(middle, gain_second))
    gate_lin = low_back(product(normed_two, w_gate))
    upward = low_back(product(normed_two, w_up))
    hidden = low(jax.nn.silu(gate_lin) * upward)
    return middle + low_back(product(hidden, w_down))

def forward(params, tokens_f, lengths):

    def one_sequence(inputs):
        return layer_sequence(params, inputs[0], inputs[1])
    return lax.map(jax.checkpoint(one_sequence), (tokens_f, lengths))

def reference(tokens, cotangent, lengths, owner_slot, master, moment_first, moment_second, basis_left, basis_right, small_master, small_first, small_second):
    matrices = assemble(low(master[owner_slot]))
    params = tuple(matrices) + tuple(split_small(low(small_master)))
    tokens_f = tokens.astype(jnp.float32)
    valid_rows = (jnp.arange(LEN, dtype=jnp.int32)[None, :] < lengths[:, None]).astype(jnp.float32)
    seed_grad = cotangent.astype(jnp.float32) * valid_rows[:, :, None]

    def run_layer(param_set, inputs):
        return forward(param_set, inputs, lengths)
    output, pullback = jax.vjp(run_layer, params, tokens_f)
    param_grads, token_grads = pullback(seed_grad)
    slot_grads = jnp.zeros((SLOTS, BLOCK, BLOCK), jnp.float32).at[owner_slot].set(disassemble(list(param_grads[:7])))
    small_grads = jnp.concatenate(list(param_grads[7:]))
    rotated = jnp.einsum('sji,sjk->sik', basis_left, slot_grads, precision=TOP_PRECISION)
    rotated = jnp.einsum('sik,skl->sil', rotated, basis_right, precision=TOP_PRECISION)
    first_new = BETA_FIRST * moment_first + (1.0 - BETA_FIRST) * rotated
    second_new = BETA_SECOND * moment_second + (1.0 - BETA_SECOND) * rotated * rotated
    normalized = first_new / (jnp.sqrt(second_new) + ADAM_EPS)
    update = jnp.einsum('sik,skl->sil', basis_left, normalized, precision=TOP_PRECISION)
    update = jnp.einsum('sik,slk->sil', update, basis_right, precision=TOP_PRECISION)
    tile_scale = jnp.sqrt(lax.optimization_barrier(jnp.mean(master * master, axis=(1, 2), keepdims=True)) + SCALE_EPS)
    master_new = master - RELATIVE_RATE * tile_scale * (update + WEIGHT_DECAY * master)
    small_first_new = BETA_FIRST * small_first + (1.0 - BETA_FIRST) * small_grads
    small_second_new = BETA_SECOND * small_second + (1.0 - BETA_SECOND) * small_grads * small_grads
    small_new = small_master - SMALL_RATE * (small_first_new / (jnp.sqrt(small_second_new) + ADAM_EPS) + WEIGHT_DECAY * small_master)
    return (output.astype(jnp.bfloat16), token_grads, first_new, second_new, master_new, small_first_new, small_second_new, small_new)
```

```python
import math

import jax
import jax.numpy as jnp
import numpy as np
from jax import lax
from jax.sharding import PartitionSpec as P

D = 1536
QH = 12
KVH = 2
HD = 128
FF = 8960
BLOCK = 128
QW = 1536
KVW = 256
N_TILES = 2856


NORM_EPS = 1e-06
ROPE_BASE = 1000000.0
BETA_FIRST = 0.5
BETA_SECOND = 0.5
ADAM_EPS = 1e-08
SCALE_EPS = 1e-06
RELATIVE_RATE = 0.5
SMALL_RATE = 0.25
WEIGHT_DECAY = 0.01
MASK_FILL = -1e30
TOP_PRECISION = lax.Precision.DEFAULT


def matrix_shapes():
    return [(D, QW), (D, KVW), (D, KVW), (QW, D), (D, FF), (D, FF), (FF, D)]


def split_small(vector):
    edges = [0, D, 2 * D, 2 * D + QW, 2 * D + QW + KVW, 2 * D + QW + 2 * KVW]
    return [vector[edges[number] : edges[number + 1]] for number in range(5)]


def arrange(slot_copies, small_copies, owner_slot):
    matrices = []
    offset = 0
    for row_count, col_count in matrix_shapes():
        tile_count = row_count // BLOCK * (col_count // BLOCK)
        picked = jnp.take(slot_copies, owner_slot[offset : offset + tile_count], axis=0)
        blocked = picked.reshape(row_count // BLOCK, col_count // BLOCK, BLOCK, BLOCK)
        matrices.append(blocked.transpose(0, 2, 1, 3).reshape(row_count, col_count))
        offset = offset + tile_count
    smalls = [member.astype(jnp.float32) for member in split_small(small_copies)]
    return (matrices, smalls)


def tile_tables():
    left_bases = [0, 0, 0, D // BLOCK, (D + QW) // BLOCK, (D + QW) // BLOCK, (2 * D + QW) // BLOCK]
    right_bases = [
        0,
        QW // BLOCK,
        (QW + KVW) // BLOCK,
        (QW + 2 * KVW) // BLOCK,
        (QW + 2 * KVW + D) // BLOCK,
        (QW + 2 * KVW + D + FF) // BLOCK,
        (QW + 2 * KVW + D + 2 * FF) // BLOCK,
    ]
    left_list = []
    right_list = []
    for number, shape_pair in enumerate(matrix_shapes()):
        grid_rows, grid_cols = np.meshgrid(
            np.arange(shape_pair[0] // BLOCK), np.arange(shape_pair[1] // BLOCK), indexing="ij"
        )
        left_list.append(left_bases[number] + grid_rows.reshape(-1))
        right_list.append(right_bases[number] + grid_cols.reshape(-1))
    return (np.concatenate(left_list).astype(np.int32), np.concatenate(right_list).astype(np.int32))


def rotate(values, positions, direction):
    half_size = HD // 2
    frequency = ROPE_BASE ** (-2.0 * jnp.arange(half_size, dtype=jnp.float32) / HD)
    angles = positions.astype(jnp.float32)[:, None] * frequency[None, :]
    cosine = jnp.cos(angles)[:, None, :]
    sine = direction * jnp.sin(angles)[:, None, :]
    first_half = values[..., :half_size]
    second_half = values[..., half_size:]
    return jnp.concatenate(
        [first_half * cosine - second_half * sine, second_half * cosine + first_half * sine],
        axis=-1,
    )


def forward_product(left_side, weight):
    return jnp.dot(left_side, weight, preferred_element_type=jnp.float32)


def back_product(grads, weight):
    return jnp.einsum("nf,df->nd", grads, weight, preferred_element_type=jnp.float32)


def outer_blocks(values):
    return values.reshape(values.shape[0], -1, BLOCK).transpose(1, 0, 2)


def norm_backward(values, inverse, gain, grad_normed):
    scaled = values * inverse
    gained = grad_normed * gain
    grad_values = inverse * (gained - scaled * jnp.mean(gained * scaled, axis=-1, keepdims=True))
    return (grad_values, jnp.sum(grad_normed * scaled, axis=0))


def local(
    tokens,
    cotangent,
    lengths,
    owner_slot,
    master,
    moment_first,
    moment_second,
    basis_left,
    basis_right,
    small_master,
    small_first,
    small_second,
):
    uly_count = lax.axis_size("uly")
    blk_count = lax.axis_size("blk")
    all_count = lax.axis_size("dp") * blk_count * uly_count
    uly_index = lax.axis_index("uly")
    blk_index = lax.axis_index("blk")
    seq_count = tokens.shape[0]
    rows_local = tokens.shape[1]
    token_count = seq_count * rows_local
    span_rows = rows_local * uly_count
    heads_local = QH // uly_count
    slot_local = master.shape[0]
    slot_total = slot_local * all_count
    score_root = math.sqrt(HD)
    positions = (blk_index * uly_count + uly_index) * rows_local + jnp.arange(
        rows_local, dtype=jnp.int32
    )
    query_pos = blk_index * span_rows + jnp.arange(span_rows, dtype=jnp.int32)
    key_head = uly_index * heads_local // (QH // KVH)
    head_pick = (jnp.arange(KVH, dtype=jnp.int32) == key_head).astype(jnp.float32)
    slot_copies, small_copies = (
        lax.all_gather(master.astype(jnp.bfloat16), ("dp", "blk", "uly"), axis=0, tiled=True),
        lax.all_gather(small_master.astype(jnp.bfloat16), ("dp", "blk", "uly"), axis=0, tiled=True),
    )
    matrices, smalls = arrange(slot_copies, small_copies, owner_slot)
    w_query, w_key, w_value, w_out, w_gate, w_up, w_down = matrices
    gain_first, gain_second, bias_query, bias_key, bias_value = smalls
    token_rows = tokens.reshape(token_count, D).astype(jnp.float32)
    inverse_first = lax.rsqrt(jnp.mean(token_rows * token_rows, axis=-1, keepdims=True) + NORM_EPS)
    normed = (token_rows * inverse_first * gain_first).astype(jnp.bfloat16)
    query_lin = forward_product(normed, w_query) + bias_query
    key_lin = forward_product(normed, w_key) + bias_key
    value_rows = (
        (forward_product(normed, w_value) + bias_value)
        .astype(jnp.bfloat16)
        .reshape(seq_count, rows_local, KVH, HD)
    )
    query_rot = rotate(query_lin.reshape(seq_count, rows_local, QH, HD), positions, 1.0).astype(
        jnp.bfloat16
    )
    key_rot = rotate(key_lin.reshape(seq_count, rows_local, KVH, HD), positions, 1.0).astype(
        jnp.bfloat16
    )
    query_heads = lax.all_to_all(query_rot, "uly", split_axis=2, concat_axis=1, tiled=True)
    key_span, value_span = (
        lax.all_gather(key_rot, "uly", axis=1, tiled=True),
        lax.all_gather(value_rows, "uly", axis=1, tiled=True),
    )

    def score_block(key_piece, first_row):
        key_sel = lax.dynamic_index_in_dim(key_piece, key_head, 2, keepdims=False)
        scores = (
            jnp.einsum("sqhd,skd->sqhk", query_heads, key_sel, preferred_element_type=jnp.float32)
            / score_root
        )
        key_pos = first_row + jnp.arange(key_piece.shape[1], dtype=jnp.int32)
        causal = key_pos[None, :] <= query_pos[:, None]
        inside = key_pos[None, :] < lengths[:, None]
        allowed = causal[None, :, None, :] & inside[:, None, None, :]
        return (scores, allowed)

    def forward_fold(carried, arrived, first_row):
        running_max, running_sum, accumulated = carried
        key_piece, value_piece = arrived
        scores, allowed = score_block(key_piece, first_row)
        new_max = jnp.maximum(running_max, jnp.max(jnp.where(allowed, scores, MASK_FILL), axis=-1))
        probs = jnp.where(allowed, jnp.exp(scores - new_max[..., None]), 0.0)
        factor = jnp.exp(running_max - new_max)
        value_sel = lax.dynamic_index_in_dim(value_piece, key_head, 2, keepdims=False).astype(
            jnp.float32
        )
        accumulated = accumulated * factor[..., None] + jnp.einsum(
            "sqhk,skd->sqhd", probs, value_sel, precision=TOP_PRECISION
        )
        return (new_max, running_sum * factor + jnp.sum(probs, axis=-1), accumulated)

    def fold_whole(step_fn, initial, whole_set):

        def one_step(step_index, carried):
            first_row = step_index * span_rows
            arrived = tuple(
                (lax.dynamic_slice_in_dim(member, first_row, span_rows, 1) for member in whole_set)
            )
            return step_fn(carried, arrived, first_row)

        return lax.fori_loop(0, blk_count, one_step, initial)

    stat_shape = (seq_count, span_rows, heads_local)
    forward_start = (
        jnp.full(stat_shape, MASK_FILL, jnp.float32),
        jnp.zeros(stat_shape, jnp.float32),
        jnp.zeros(stat_shape + (HD,), jnp.float32),
    )
    key_whole, value_whole = (
        lax.all_gather(key_span, "blk", axis=1, tiled=True),
        lax.all_gather(value_span, "blk", axis=1, tiled=True),
    )
    running_max, running_sum, accumulated = fold_whole(
        forward_fold, forward_start, (key_whole, value_whole)
    )
    attended = accumulated / running_sum[..., None]
    log_sum = running_max + jnp.log(running_sum)
    out_rows = lax.all_to_all(
        attended.astype(jnp.bfloat16), "uly", split_axis=1, concat_axis=2, tiled=True
    ).reshape(token_count, QW)
    middle = token_rows + forward_product(out_rows, w_out)
    inverse_second = lax.rsqrt(jnp.mean(middle * middle, axis=-1, keepdims=True) + NORM_EPS)
    normed_two = (middle * inverse_second * gain_second).astype(jnp.bfloat16)
    gate_lin = forward_product(normed_two, w_gate)
    upward = forward_product(normed_two, w_up)
    hidden = (jax.nn.silu(gate_lin) * upward).astype(jnp.bfloat16)
    mixed_out = (
        (middle + forward_product(hidden, w_down))
        .astype(jnp.bfloat16)
        .reshape(seq_count, rows_local, D)
    )
    valid_rows = (positions[None, :] < lengths[:, None]).astype(jnp.float32)
    seed_grad = (cotangent.astype(jnp.float32) * valid_rows[:, :, None]).reshape(token_count, D)
    seed_low = seed_grad.astype(jnp.bfloat16)
    grad_hidden = back_product(seed_low, w_down)
    gate_sigmoid = jax.nn.sigmoid(gate_lin)
    grad_gate = (
        grad_hidden * upward * gate_sigmoid * (1.0 + gate_lin * (1.0 - gate_sigmoid))
    ).astype(jnp.bfloat16)
    grad_up = (grad_hidden * gate_lin * gate_sigmoid).astype(jnp.bfloat16)
    grad_normed_two = back_product(grad_gate, w_gate) + back_product(grad_up, w_up)
    norm_part_two, gain_second_grad = norm_backward(
        middle, inverse_second, gain_second, grad_normed_two
    )
    grad_middle = seed_grad + norm_part_two
    grad_middle_low = grad_middle.astype(jnp.bfloat16)
    grad_out_rows = (
        back_product(grad_middle_low, w_out)
        .astype(jnp.bfloat16)
        .reshape(seq_count, rows_local, QH, HD)
    )
    grad_heads = lax.all_to_all(grad_out_rows, "uly", split_axis=2, concat_axis=1, tiled=True)
    grad_heads_wide = grad_heads.astype(jnp.float32)
    row_delta = jnp.sum(grad_heads_wide * attended, axis=-1)

    def backward_fold(carried, arrived, first_row):
        grad_query, grad_keys, grad_values = carried
        key_piece, value_piece = arrived
        scores, allowed = score_block(key_piece, first_row)
        probs = jnp.where(allowed, jnp.exp(scores - log_sum[..., None]), 0.0)
        value_sel = lax.dynamic_index_in_dim(value_piece, key_head, 2, keepdims=False)
        key_sel = lax.dynamic_index_in_dim(key_piece, key_head, 2, keepdims=False)
        grad_prob = jnp.einsum(
            "sqhd,skd->sqhk", grad_heads, value_sel, preferred_element_type=jnp.float32
        )
        grad_score = (probs * (grad_prob - row_delta[..., None])).astype(jnp.bfloat16)
        grad_query = grad_query + jnp.einsum(
            "sqhk,skd->sqhd", grad_score, key_sel, preferred_element_type=jnp.float32
        )
        key_part = jnp.einsum(
            "sqhk,sqhd->skd", grad_score, query_heads, preferred_element_type=jnp.float32
        )
        value_part = jnp.einsum("sqhk,sqhd->skd", probs, grad_heads_wide, precision=TOP_PRECISION)
        key_part = key_part[:, :, None, :] * head_pick[None, None, :, None]
        value_part = value_part[:, :, None, :] * head_pick[None, None, :, None]
        grad_keys = lax.dynamic_update_slice_in_dim(grad_keys, key_part, first_row, 1)
        grad_values = lax.dynamic_update_slice_in_dim(grad_values, value_part, first_row, 1)
        return (grad_query, grad_keys, grad_values)

    kv_shape = (seq_count, span_rows * blk_count, KVH, HD)
    backward_start = (
        jnp.zeros(stat_shape + (HD,), jnp.float32),
        jnp.zeros(kv_shape, jnp.float32),
        jnp.zeros(kv_shape, jnp.float32),
    )
    grad_query, grad_keys, grad_values = fold_whole(
        backward_fold, backward_start, (key_whole, value_whole)
    )
    grad_query_low = (grad_query / score_root).astype(jnp.bfloat16)
    grad_query_rows = lax.all_to_all(grad_query_low, "uly", split_axis=1, concat_axis=2, tiled=True)
    grad_keys_span, grad_values_span = (
        lax.psum_scatter(
            (grad_keys / score_root).astype(jnp.bfloat16), "blk", scatter_dimension=1, tiled=True
        ).astype(jnp.float32),
        lax.psum_scatter(
            grad_values.astype(jnp.bfloat16), "blk", scatter_dimension=1, tiled=True
        ).astype(jnp.float32),
    )
    grad_keys_rows, grad_values_rows = (
        lax.psum_scatter(grad_keys_span, "uly", scatter_dimension=1, tiled=True),
        lax.psum_scatter(grad_values_span, "uly", scatter_dimension=1, tiled=True),
    )
    grad_query_lin = (
        rotate(grad_query_rows.astype(jnp.float32), positions, -1.0)
        .astype(jnp.bfloat16)
        .reshape(token_count, QW)
    )
    key_rounded = lax.optimization_barrier(grad_keys_rows.astype(jnp.bfloat16)).astype(jnp.float32)
    grad_key_lin = (
        rotate(key_rounded, positions, -1.0).astype(jnp.bfloat16).reshape(token_count, KVW)
    )
    grad_value_lin = grad_values_rows.astype(jnp.bfloat16).reshape(token_count, KVW)
    grad_normed = (
        back_product(grad_query_lin, w_query)
        + back_product(grad_key_lin, w_key)
        + back_product(grad_value_lin, w_value)
    )
    norm_part_first, gain_first_grad = norm_backward(
        token_rows, inverse_first, gain_first, grad_normed
    )
    grad_tokens = (grad_middle + norm_part_first).reshape(seq_count, rows_local, D)
    small_partial = jnp.concatenate(
        [
            gain_first_grad,
            gain_second_grad,
            jnp.sum(grad_query_lin, axis=0, dtype=jnp.float32),
            jnp.sum(grad_key_lin, axis=0, dtype=jnp.float32),
            jnp.sum(grad_value_lin, axis=0, dtype=jnp.float32),
        ]
    )
    grad_small = lax.psum_scatter(
        small_partial, ("dp", "blk", "uly"), scatter_dimension=0, tiled=True
    )
    left_table = jnp.concatenate(
        [
            outer_blocks(normed),
            outer_blocks(out_rows),
            outer_blocks(normed_two),
            outer_blocks(hidden),
        ],
        axis=0,
    )
    right_table = jnp.concatenate(
        [
            outer_blocks(grad_query_lin),
            outer_blocks(grad_key_lin),
            outer_blocks(grad_value_lin),
            outer_blocks(grad_middle_low),
            outer_blocks(grad_gate),
            outer_blocks(grad_up),
            outer_blocks(seed_low),
        ],
        axis=0,
    )
    left_ids, right_ids = tile_tables()
    tile_of_slot = (
        jnp.zeros((slot_total,), jnp.int32).at[owner_slot].set(jnp.arange(N_TILES, dtype=jnp.int32))
    )
    slot_used = jnp.zeros((slot_total,), jnp.float32).at[owner_slot].set(1.0)
    slot_left = jnp.take(jnp.asarray(left_ids), tile_of_slot)
    slot_right = jnp.take(jnp.asarray(right_ids), tile_of_slot)
    row_ids = jnp.arange(lax.axis_size(("dp", "blk", "uly")) * slot_local, dtype=jnp.int32)
    global_ids = row_ids // slot_local * slot_local + row_ids % slot_local
    left_part = jnp.take(left_table, jnp.take(slot_left, global_ids), axis=0)
    right_part = jnp.take(right_table, jnp.take(slot_right, global_ids), axis=0)
    used_mask = jnp.take(slot_used, global_ids)
    grad_slots = lax.psum_scatter(
        (
            jnp.einsum("snb,snc->sbc", left_part, right_part, preferred_element_type=jnp.float32)
            * used_mask[:, None, None]
        ).astype(jnp.bfloat16),
        ("dp", "blk", "uly"),
        scatter_dimension=0,
        tiled=True,
    ).astype(jnp.float32)
    rotated = jnp.einsum("sji,sjk->sik", basis_left, grad_slots, precision=TOP_PRECISION)
    rotated = jnp.einsum("sik,skl->sil", rotated, basis_right, precision=TOP_PRECISION)
    first_new = BETA_FIRST * moment_first + (1.0 - BETA_FIRST) * rotated
    second_new = BETA_SECOND * moment_second + (1.0 - BETA_SECOND) * rotated * rotated
    normalized = first_new / (jnp.sqrt(second_new) + ADAM_EPS)
    update = jnp.einsum("sik,skl->sil", basis_left, normalized, precision=TOP_PRECISION)
    update = jnp.einsum("sik,slk->sil", update, basis_right, precision=TOP_PRECISION)
    tile_scale = jnp.sqrt(jnp.mean(master * master, axis=(1, 2), keepdims=True) + SCALE_EPS)
    master_new = master - RELATIVE_RATE * tile_scale * (update + WEIGHT_DECAY * master)
    small_first_new = BETA_FIRST * small_first + (1.0 - BETA_FIRST) * grad_small
    small_second_new = BETA_SECOND * small_second + (1.0 - BETA_SECOND) * grad_small * grad_small
    small_new = small_master - SMALL_RATE * (
        small_first_new / (jnp.sqrt(small_second_new) + ADAM_EPS) + WEIGHT_DECAY * small_master
    )
    return (
        mixed_out,
        grad_tokens,
        first_new,
        second_new,
        master_new,
        small_first_new,
        small_second_new,
        small_new,
    )


def solution(mesh):
    in_specs = (
        P("dp", ("blk", "uly"), None),
        P("dp", ("blk", "uly"), None),
        P("dp"),
        P(),
        P(("dp", "blk", "uly"), None, None),
        P(("dp", "blk", "uly"), None, None),
        P(("dp", "blk", "uly"), None, None),
        P(("dp", "blk", "uly"), None, None),
        P(("dp", "blk", "uly"), None, None),
        P(("dp", "blk", "uly")),
        P(("dp", "blk", "uly")),
        P(("dp", "blk", "uly")),
    )
    out_specs = (
        P("dp", ("blk", "uly"), None),
        P("dp", ("blk", "uly"), None),
        P(("dp", "blk", "uly"), None, None),
        P(("dp", "blk", "uly"), None, None),
        P(("dp", "blk", "uly"), None, None),
        P(("dp", "blk", "uly")),
        P(("dp", "blk", "uly")),
        P(("dp", "blk", "uly")),
    )
    return jax.shard_map(local, mesh=mesh, in_specs=in_specs, out_specs=out_specs, check_vma=False)
```

```python
import math

import jax
import jax.numpy as jnp
import numpy as np
from jax import lax
from jax.sharding import PartitionSpec as P

D = 1536
QH = 12
KVH = 2
HD = 128
FF = 8960
BLOCK = 128
QW = 1536
KVW = 256


NORM_EPS = 1e-06
ROPE_BASE = 1000000.0
BETA_FIRST = 0.5
BETA_SECOND = 0.5
ADAM_EPS = 1e-08
SCALE_EPS = 1e-06
RELATIVE_RATE = 0.5
SMALL_RATE = 0.25
WEIGHT_DECAY = 0.01
MASK_FILL = -1e30
TOP_PRECISION = lax.Precision.DEFAULT


def matrix_shapes():
    return [(D, QW), (D, KVW), (D, KVW), (QW, D), (D, FF), (D, FF), (FF, D)]


def split_small(vector):
    edges = [0, D, 2 * D, 2 * D + QW, 2 * D + QW + KVW, 2 * D + QW + 2 * KVW]
    return [vector[edges[number] : edges[number + 1]] for number in range(5)]


GRID_D = D // BLOCK
GRID_FF = FF // BLOCK
ATTN_TILES = GRID_D * (QW + 2 * KVW) // BLOCK + QW // BLOCK * GRID_D
ALL_AXES = ("dp", "blk", "uly")
COLUMN_AXES = ("dp", "uly")


def capacity(mean, factor, limit):
    return int(min(limit, math.ceil(mean + factor * math.sqrt(mean))))


def pick(table, index):
    return jnp.take(table, index, axis=0, mode="clip")


def earlier_equal(keys):
    number = jnp.arange(keys.shape[0], dtype=jnp.int32)
    same = keys[None, :] == keys[:, None]
    return jnp.sum((same & (number[None, :] < number[:, None])).astype(jnp.int32), axis=1)


def locate(wanted, keys, values):
    return jnp.sum(jnp.where(wanted[:, None] == keys[None, :], values[None, :], 0), axis=1)


def tiles_to_matrix(tiles, row_tiles, col_tiles):
    blocked = tiles.reshape(row_tiles, col_tiles, BLOCK, BLOCK)
    return blocked.transpose(0, 2, 1, 3).reshape(row_tiles * BLOCK, col_tiles * BLOCK)


def matrix_to_tiles(matrix):
    row_tiles = matrix.shape[0] // BLOCK
    col_tiles = matrix.shape[1] // BLOCK
    blocked = matrix.reshape(row_tiles, BLOCK, col_tiles, BLOCK)
    return blocked.transpose(0, 2, 1, 3).reshape(row_tiles * col_tiles, BLOCK, BLOCK)


def exchange(values, axes):
    return lax.all_to_all(values, axes, split_axis=0, concat_axis=0, tiled=True)


def spread(values, axes):
    count = lax.axis_size(axes)
    return exchange(jnp.broadcast_to(values[None], (count,) + values.shape), axes)


def exchange_sum(values, axes):
    return jnp.sum(exchange(values, axes).astype(jnp.float32), axis=0)


def shard_owners(owner_slot, shard_count, shard_groups):
    padded = shard_count * shard_groups
    first = ATTN_TILES
    members = []
    for _ in range(2):
        grid = owner_slot[first : first + GRID_D * GRID_FF].reshape(GRID_D, GRID_FF)
        grid = jnp.pad(grid, ((0, 0), (0, padded - GRID_FF)), constant_values=-1)
        members.append(
            grid.reshape(GRID_D, shard_count, shard_groups).transpose(1, 0, 2).reshape(shard_count, -1)
        )
        first = first + GRID_D * GRID_FF
    grid = owner_slot[first : first + GRID_D * GRID_FF].reshape(GRID_FF, GRID_D)
    grid = jnp.pad(grid, ((0, padded - GRID_FF), (0, 0)), constant_values=-1)
    members.append(grid.reshape(shard_count, -1))
    return jnp.concatenate(members, axis=1)


def rotate(values, positions, direction):
    half_size = HD // 2
    frequency = ROPE_BASE ** (-2.0 * jnp.arange(half_size, dtype=jnp.float32) / HD)
    angles = positions.astype(jnp.float32)[:, None] * frequency[None, :]
    cosine = jnp.cos(angles)[:, None, :]
    sine = direction * jnp.sin(angles)[:, None, :]
    first_half = values[..., :half_size]
    second_half = values[..., half_size:]
    return jnp.concatenate(
        [first_half * cosine - second_half * sine, second_half * cosine + first_half * sine],
        axis=-1,
    )


def forward_product(left_side, weight):
    return jnp.dot(left_side, weight, preferred_element_type=jnp.float32)


def back_product(grads, weight):
    return jnp.einsum("nf,df->nd", grads, weight, preferred_element_type=jnp.float32)


def outer_product(left_side, right_side):
    return jnp.einsum(
        "nb,nc->bc", left_side, right_side, preferred_element_type=jnp.float32
    ).astype(jnp.bfloat16)


def norm_backward(values, inverse, gain, grad_normed):
    scaled = values * inverse
    gained = grad_normed * gain
    grad_values = inverse * (gained - scaled * jnp.mean(gained * scaled, axis=-1, keepdims=True))
    return (grad_values, jnp.sum(grad_normed * scaled, axis=0))


def local(
    tokens,
    cotangent,
    lengths,
    owner_slot,
    master,
    moment_first,
    moment_second,
    basis_left,
    basis_right,
    small_master,
    small_first,
    small_second,
):
    uly_count = lax.axis_size("uly")
    blk_count = lax.axis_size("blk")
    all_count = lax.axis_size("dp") * blk_count * uly_count
    uly_index = lax.axis_index("uly")
    blk_index = lax.axis_index("blk")
    seq_count = tokens.shape[0]
    rows_local = tokens.shape[1]
    token_count = seq_count * rows_local
    span_rows = rows_local * uly_count
    heads_local = QH // uly_count
    slot_local = master.shape[0]
    slot_total = slot_local * all_count
    score_root = math.sqrt(HD)
    positions = (blk_index * uly_count + uly_index) * rows_local + jnp.arange(
        rows_local, dtype=jnp.int32
    )
    query_pos = blk_index * span_rows + jnp.arange(span_rows, dtype=jnp.int32)
    head_of = [member * heads_local // (QH // KVH) for member in range(uly_count)]
    dp_index = lax.axis_index("dp")
    my_device = (dp_index * blk_count + blk_index) * uly_count + uly_index
    my_column = dp_index * uly_count + uly_index
    column_count = lax.axis_size("dp") * uly_count
    shard_groups = -(-GRID_FF // blk_count)
    shard_tiles = 3 * GRID_D * shard_groups
    pair_cap = capacity(shard_tiles / all_count, 3.5, slot_local)
    column_cap = capacity(shard_tiles / column_count, 3.45, shard_tiles)
    attn_cap = capacity(ATTN_TILES / all_count, 3.8, slot_local)

    owners = shard_owners(owner_slot, blk_count, shard_groups)
    owner_flat = owners.reshape(-1)
    real_flat = owner_flat >= 0
    shard_flat = jnp.repeat(jnp.arange(blk_count, dtype=jnp.int32), shard_tiles)
    device_flat = jnp.maximum(owner_flat, 0) // slot_local
    column_flat = device_flat // (blk_count * uly_count) * uly_count + device_flat % uly_count
    source_flat = device_flat // uly_count % blk_count
    pair_flat = jnp.where(real_flat, device_flat * blk_count + shard_flat, -1)
    line_flat = jnp.where(real_flat, column_flat * blk_count + shard_flat, -1)
    pair_rank = earlier_equal(pair_flat)
    line_rank = earlier_equal(line_flat)
    attn_owner = owner_slot[:ATTN_TILES]
    attn_device = attn_owner // slot_local
    attn_rank = earlier_equal(attn_device)
    fits_shards = (jnp.max(jnp.where(real_flat, pair_rank, 0)) < pair_cap) & (
        jnp.max(jnp.where(real_flat, line_rank, 0)) < column_cap
    )
    fits_attn = jnp.max(attn_rank) < attn_cap
    my_first = my_device * slot_local

    def mine(flat):
        return lax.dynamic_slice_in_dim(flat, blk_index * shard_tiles, shard_tiles, 0)

    my_real = mine(real_flat)
    my_owner = mine(owner_flat)
    my_source = mine(source_flat)
    my_pair_rank = mine(pair_rank)
    my_line_rank = mine(line_rank)
    my_columns = mine(column_flat)
    in_column = my_real & (my_columns == my_column)
    place = jnp.where(my_real, my_columns * column_cap + my_line_rank, -1)
    send_key = jnp.where(
        real_flat & (device_flat == my_device) & (pair_rank < pair_cap),
        shard_flat * pair_cap + pair_rank,
        -1,
    )
    pair_slots = jnp.arange(blk_count * pair_cap, dtype=jnp.int32)
    send_index = locate(pair_slots, send_key, owner_flat - my_first)
    arrival = my_source * pair_cap + my_pair_rank
    fits_pair = my_pair_rank < pair_cap
    compact_index = locate(
        jnp.arange(column_cap, dtype=jnp.int32),
        jnp.where(in_column & fits_pair, my_line_rank, -1),
        arrival,
    )
    attn_send = locate(
        jnp.arange(attn_cap, dtype=jnp.int32),
        jnp.where(attn_device == my_device, attn_rank, -1),
        attn_owner - my_first,
    )
    attn_place = attn_device * attn_cap + attn_rank

    master_low = master.astype(jnp.bfloat16)
    small_copies = spread(small_master.astype(jnp.bfloat16), ALL_AXES).reshape(-1)
    attn_buffer = lax.all_gather(pick(master_low, attn_send), ALL_AXES, axis=0, tiled=True)

    def whole_tiles(index):
        return pick(lax.all_gather(master_low, ALL_AXES, axis=0, tiled=True), index)

    attn_tiles = lax.cond(
        fits_attn, lambda: pick(attn_buffer, attn_place), lambda: whole_tiles(attn_owner)
    )
    arrived_tiles = exchange(pick(master_low, send_index), "blk")
    shard_buffer = lax.all_gather(pick(arrived_tiles, compact_index), COLUMN_AXES, axis=0, tiled=True)
    shard_stack = lax.cond(
        fits_shards, lambda: pick(shard_buffer, place), lambda: whole_tiles(my_owner)
    )
    third = GRID_D * shard_groups
    real_groups = (
        blk_index * shard_groups + jnp.arange(shard_groups, dtype=jnp.int32)
    ) < GRID_FF
    real_hidden = jnp.repeat(real_groups, BLOCK)
    w_gate = jnp.where(
        real_hidden[None, :], tiles_to_matrix(shard_stack[:third], GRID_D, shard_groups), 0
    )
    w_up = jnp.where(
        real_hidden[None, :], tiles_to_matrix(shard_stack[third : 2 * third], GRID_D, shard_groups), 0
    )
    w_down = jnp.where(
        real_hidden[:, None], tiles_to_matrix(shard_stack[2 * third :], shard_groups, GRID_D), 0
    )
    attn_matrices = []
    first = 0
    for row_count, col_count in matrix_shapes()[:4]:
        tile_count = row_count // BLOCK * (col_count // BLOCK)
        attn_matrices.append(
            tiles_to_matrix(
                attn_tiles[first : first + tile_count], row_count // BLOCK, col_count // BLOCK
            )
        )
        first = first + tile_count
    w_query, w_key, w_value, w_out = attn_matrices
    smalls = [member.astype(jnp.float32) for member in split_small(small_copies)]
    gain_first, gain_second, bias_query, bias_key, bias_value = smalls
    valid_rows = (positions[None, :] < lengths[:, None]).astype(jnp.float32)
    seed_grad = (cotangent.astype(jnp.float32) * valid_rows[:, :, None]).reshape(token_count, D)
    seed_low = seed_grad.astype(jnp.bfloat16)
    seed_line = spread(seed_low, "blk").reshape(blk_count * token_count, D)
    token_rows = tokens.reshape(token_count, D).astype(jnp.float32)
    inverse_first = lax.rsqrt(jnp.mean(token_rows * token_rows, axis=-1, keepdims=True) + NORM_EPS)
    normed = (token_rows * inverse_first * gain_first).astype(jnp.bfloat16)
    query_lin = forward_product(normed, w_query) + bias_query
    key_lin = forward_product(normed, w_key) + bias_key
    value_rows = (
        (forward_product(normed, w_value) + bias_value)
        .astype(jnp.bfloat16)
        .reshape(seq_count, rows_local, KVH, HD)
    )
    query_rot = rotate(query_lin.reshape(seq_count, rows_local, QH, HD), positions, 1.0).astype(
        jnp.bfloat16
    )
    key_rot = rotate(key_lin.reshape(seq_count, rows_local, KVH, HD), positions, 1.0).astype(
        jnp.bfloat16
    )
    query_heads = lax.all_to_all(query_rot, "uly", split_axis=2, concat_axis=1, tiled=True)
    key_value = jnp.concatenate([key_rot, value_rows], axis=-1)
    key_value = jnp.stack([key_value[:, :, head] for head in head_of], axis=0)
    key_value = exchange(key_value, "uly").transpose(1, 0, 2, 3)
    key_value = spread(key_value, "blk").transpose(1, 0, 2, 3, 4)
    key_value = key_value.reshape(seq_count, blk_count * span_rows, 2 * HD)
    keys = key_value[..., :HD]
    values = key_value[..., HD:]
    key_pos = jnp.arange(blk_count * span_rows, dtype=jnp.int32)
    allowed = (key_pos[None, None, :] <= query_pos[None, :, None]) & (
        key_pos[None, None, :] < lengths[:, None, None]
    )
    allowed = allowed[:, :, None, :]
    scores = (
        jnp.einsum("sqhd,skd->sqhk", query_heads, keys, preferred_element_type=jnp.float32)
        / score_root
    )
    scores = jnp.where(allowed, scores, MASK_FILL)
    top = jnp.max(scores, axis=-1, keepdims=True)
    weights = jnp.where(allowed, jnp.exp(scores - top), 0.0)
    probs = weights / jnp.sum(weights, axis=-1, keepdims=True)
    probs_low = probs.astype(jnp.bfloat16)
    attended = jnp.einsum(
        "sqhk,skd->sqhd", probs_low, values, preferred_element_type=jnp.float32
    )
    out_rows = lax.all_to_all(
        attended.astype(jnp.bfloat16), "uly", split_axis=1, concat_axis=2, tiled=True
    ).reshape(token_count, QW)
    middle = token_rows + forward_product(out_rows, w_out)
    inverse_second = lax.rsqrt(jnp.mean(middle * middle, axis=-1, keepdims=True) + NORM_EPS)
    normed_two = (middle * inverse_second * gain_second).astype(jnp.bfloat16)
    normed_line = spread(normed_two, "blk").reshape(blk_count * token_count, D)
    gate_lin = forward_product(normed_line, w_gate)
    upward = forward_product(normed_line, w_up)
    hidden = (jax.nn.silu(gate_lin) * upward).astype(jnp.bfloat16)
    grad_hidden = back_product(seed_line, w_down)
    gate_sigmoid = jax.nn.sigmoid(gate_lin)
    grad_gate = (
        grad_hidden * upward * gate_sigmoid * (1.0 + gate_lin * (1.0 - gate_sigmoid))
    ).astype(jnp.bfloat16)
    grad_up = (grad_hidden * gate_lin * gate_sigmoid).astype(jnp.bfloat16)
    grad_line = back_product(grad_gate, w_gate) + back_product(grad_up, w_up)
    grad_normed_two = exchange_sum(
        grad_line.astype(jnp.bfloat16).reshape(blk_count, token_count, D), "blk"
    )
    mixed_line = forward_product(hidden, w_down).astype(jnp.bfloat16)
    mixed_out = (
        (middle + exchange_sum(mixed_line.reshape(blk_count, token_count, D), "blk"))
        .astype(jnp.bfloat16)
        .reshape(seq_count, rows_local, D)
    )
    shard_grads = jnp.concatenate(
        [
            matrix_to_tiles(outer_product(normed_line, grad_gate)),
            matrix_to_tiles(outer_product(normed_line, grad_up)),
            matrix_to_tiles(outer_product(hidden, seed_line)),
        ],
        axis=0,
    )
    scatter_index = locate(
        jnp.arange(column_count * column_cap, dtype=jnp.int32),
        place,
        jnp.arange(shard_tiles, dtype=jnp.int32),
    )
    column_grads = lax.psum_scatter(
        pick(shard_grads, scatter_index), COLUMN_AXES, scatter_dimension=0, tiled=True
    )
    return_key = jnp.where(in_column & fits_pair, arrival, -1)
    returned_grads = exchange(pick(column_grads, locate(pair_slots, return_key, my_line_rank)), "blk")
    norm_part_two, gain_second_grad = norm_backward(
        middle, inverse_second, gain_second, grad_normed_two
    )
    grad_middle = seed_grad + norm_part_two
    grad_middle_low = grad_middle.astype(jnp.bfloat16)
    grad_out_rows = (
        back_product(grad_middle_low, w_out)
        .astype(jnp.bfloat16)
        .reshape(seq_count, rows_local, QH, HD)
    )
    grad_heads = lax.all_to_all(grad_out_rows, "uly", split_axis=2, concat_axis=1, tiled=True)
    grad_heads_wide = grad_heads.astype(jnp.float32)
    row_delta = jnp.sum(grad_heads_wide * attended, axis=-1)

    grad_prob = jnp.einsum(
        "sqhd,skd->sqhk", grad_heads, values, preferred_element_type=jnp.float32
    )
    grad_score = (probs * (grad_prob - row_delta[..., None])).astype(jnp.bfloat16)
    grad_query = jnp.einsum(
        "sqhk,skd->sqhd", grad_score, keys, preferred_element_type=jnp.float32
    )
    grad_keys = jnp.einsum(
        "sqhk,sqhd->skd", grad_score, query_heads, preferred_element_type=jnp.float32
    )
    grad_values = jnp.einsum(
        "sqhk,sqhd->skd", probs_low, grad_heads, preferred_element_type=jnp.float32
    )
    grad_query_low = (grad_query / score_root).astype(jnp.bfloat16)
    grad_query_rows = lax.all_to_all(grad_query_low, "uly", split_axis=1, concat_axis=2, tiled=True)
    grad_pair = jnp.concatenate([grad_keys / score_root, grad_values], axis=-1).astype(jnp.bfloat16)
    grad_pair = grad_pair.reshape(seq_count, blk_count, span_rows, 2 * HD).transpose(1, 0, 2, 3)
    grad_pair = exchange_sum(grad_pair, "blk").astype(jnp.bfloat16)
    grad_pair = grad_pair.reshape(seq_count, uly_count, rows_local, 2 * HD).transpose(1, 0, 2, 3)
    grad_pair = exchange(grad_pair, "uly").astype(jnp.float32)
    grad_pair = jnp.stack(
        [
            sum(grad_pair[member] for member in range(uly_count) if head_of[member] == head)
            for head in range(KVH)
        ],
        axis=2,
    )
    grad_keys_rows = grad_pair[..., :HD]
    grad_values_rows = grad_pair[..., HD:]
    grad_query_lin = (
        rotate(grad_query_rows.astype(jnp.float32), positions, -1.0)
        .astype(jnp.bfloat16)
        .reshape(token_count, QW)
    )
    key_rounded = grad_keys_rows
    grad_key_lin = (
        rotate(key_rounded, positions, -1.0).astype(jnp.bfloat16).reshape(token_count, KVW)
    )
    grad_value_lin = grad_values_rows.astype(jnp.bfloat16).reshape(token_count, KVW)
    grad_normed = (
        back_product(grad_query_lin, w_query)
        + back_product(grad_key_lin, w_key)
        + back_product(grad_value_lin, w_value)
    )
    norm_part_first, gain_first_grad = norm_backward(
        token_rows, inverse_first, gain_first, grad_normed
    )
    grad_tokens = (grad_middle + norm_part_first).reshape(seq_count, rows_local, D)
    small_partial = jnp.concatenate(
        [
            gain_first_grad,
            gain_second_grad,
            jnp.sum(grad_query_lin, axis=0, dtype=jnp.float32),
            jnp.sum(grad_key_lin, axis=0, dtype=jnp.float32),
            jnp.sum(grad_value_lin, axis=0, dtype=jnp.float32),
        ]
    )
    grad_small = exchange_sum(small_partial.reshape(all_count, -1), ALL_AXES)
    attn_grads = jnp.concatenate(
        [
            matrix_to_tiles(outer_product(normed, grad_query_lin)),
            matrix_to_tiles(outer_product(normed, grad_key_lin)),
            matrix_to_tiles(outer_product(normed, grad_value_lin)),
            matrix_to_tiles(outer_product(out_rows, grad_middle_low)),
        ],
        axis=0,
    )
    attn_index = locate(
        jnp.arange(all_count * attn_cap, dtype=jnp.int32),
        attn_place,
        jnp.arange(ATTN_TILES, dtype=jnp.int32),
    )
    attn_returned = lax.psum_scatter(
        pick(attn_grads, attn_index), ALL_AXES, scatter_dimension=0, tiled=True
    )
    my_slots = my_first + jnp.arange(slot_local, dtype=jnp.int32)
    slot_index = locate(my_slots, owner_flat, shard_flat * pair_cap + pair_rank) + locate(
        my_slots, attn_owner, blk_count * pair_cap + attn_rank
    )
    slot_used = jnp.any(my_slots[:, None] == owner_slot[None, :], axis=1)

    def routed_grads():
        return pick(jnp.concatenate([returned_grads, attn_returned], axis=0), slot_index)

    def summed_grads():
        every_slot = jnp.arange(slot_total, dtype=jnp.int32)
        tile_owner = jnp.concatenate([my_owner, attn_owner])
        index = locate(every_slot, tile_owner, jnp.arange(tile_owner.shape[0], dtype=jnp.int32))
        held = jnp.any(every_slot[:, None] == tile_owner[None, :], axis=1)
        parts = pick(jnp.concatenate([shard_grads, attn_grads], axis=0), index)
        parts = jnp.where(held[:, None, None], parts, 0)
        return lax.psum_scatter(parts, ALL_AXES, scatter_dimension=0, tiled=True)

    grad_slots = lax.cond(fits_shards & fits_attn, routed_grads, summed_grads)
    grad_slots = jnp.where(slot_used[:, None, None], grad_slots, 0).astype(jnp.float32)
    rotated = jnp.einsum("sji,sjk->sik", basis_left, grad_slots, precision=TOP_PRECISION)
    rotated = jnp.einsum("sik,skl->sil", rotated, basis_right, precision=TOP_PRECISION)
    first_new = BETA_FIRST * moment_first + (1.0 - BETA_FIRST) * rotated
    second_new = BETA_SECOND * moment_second + (1.0 - BETA_SECOND) * rotated * rotated
    normalized = first_new / (jnp.sqrt(second_new) + ADAM_EPS)
    update = jnp.einsum("sik,skl->sil", basis_left, normalized, precision=TOP_PRECISION)
    update = jnp.einsum("sik,slk->sil", update, basis_right, precision=TOP_PRECISION)
    tile_scale = jnp.sqrt(jnp.mean(master * master, axis=(1, 2), keepdims=True) + SCALE_EPS)
    master_new = master - RELATIVE_RATE * tile_scale * (update + WEIGHT_DECAY * master)
    small_first_new = BETA_FIRST * small_first + (1.0 - BETA_FIRST) * grad_small
    small_second_new = BETA_SECOND * small_second + (1.0 - BETA_SECOND) * grad_small * grad_small
    small_new = small_master - SMALL_RATE * (
        small_first_new / (jnp.sqrt(small_second_new) + ADAM_EPS) + WEIGHT_DECAY * small_master
    )
    return (
        mixed_out,
        grad_tokens,
        first_new,
        second_new,
        master_new,
        small_first_new,
        small_second_new,
        small_new,
    )


def solution(mesh):
    in_specs = (
        P("dp", ("blk", "uly"), None),
        P("dp", ("blk", "uly"), None),
        P("dp"),
        P(),
        P(("dp", "blk", "uly"), None, None),
        P(("dp", "blk", "uly"), None, None),
        P(("dp", "blk", "uly"), None, None),
        P(("dp", "blk", "uly"), None, None),
        P(("dp", "blk", "uly"), None, None),
        P(("dp", "blk", "uly")),
        P(("dp", "blk", "uly")),
        P(("dp", "blk", "uly")),
    )
    out_specs = (
        P("dp", ("blk", "uly"), None),
        P("dp", ("blk", "uly"), None),
        P(("dp", "blk", "uly"), None, None),
        P(("dp", "blk", "uly"), None, None),
        P(("dp", "blk", "uly"), None, None),
        P(("dp", "blk", "uly")),
        P(("dp", "blk", "uly")),
        P(("dp", "blk", "uly")),
    )
    return jax.shard_map(local, mesh=mesh, in_specs=in_specs, out_specs=out_specs, check_vma=False)
```

```python
import math

import jax
import jax.numpy as jnp
import numpy as np
from jax import lax
from jax.sharding import PartitionSpec as P

D = 1536
QH = 12
KVH = 2
HD = 128
FF = 8960
BLOCK = 128
QW = 1536
KVW = 256


NORM_EPS = 1e-06
ROPE_BASE = 1000000.0
BETA_FIRST = 0.5
BETA_SECOND = 0.5
ADAM_EPS = 1e-08
SCALE_EPS = 1e-06
RELATIVE_RATE = 0.5
SMALL_RATE = 0.25
WEIGHT_DECAY = 0.01
MASK_FILL = -1e30
TOP_PRECISION = lax.Precision.DEFAULT


def matrix_shapes():
    return [(D, QW), (D, KVW), (D, KVW), (QW, D), (D, FF), (D, FF), (FF, D)]


def split_small(vector):
    edges = [0, D, 2 * D, 2 * D + QW, 2 * D + QW + KVW, 2 * D + QW + 2 * KVW]
    return [vector[edges[number] : edges[number + 1]] for number in range(5)]


GRID_D = D // BLOCK
GRID_FF = FF // BLOCK
ATTN_TILES = GRID_D * (QW + 2 * KVW) // BLOCK + QW // BLOCK * GRID_D
ALL_AXES = ("dp", "blk", "uly")
COLUMN_AXES = ("dp", "uly")


def capacity(mean, factor, limit):
    return int(min(limit, math.ceil(mean + factor * math.sqrt(mean))))


def pick(table, index):
    return jnp.take(table, index, axis=0, mode="clip")


def earlier_equal(keys):
    number = jnp.arange(keys.shape[0], dtype=jnp.int32)
    same = keys[None, :] == keys[:, None]
    return jnp.sum((same & (number[None, :] < number[:, None])).astype(jnp.int32), axis=1)


def locate(wanted, keys, values):
    return jnp.sum(jnp.where(wanted[:, None] == keys[None, :], values[None, :], 0), axis=1)


def tiles_to_matrix(tiles, row_tiles, col_tiles):
    blocked = tiles.reshape(row_tiles, col_tiles, BLOCK, BLOCK)
    return blocked.transpose(0, 2, 1, 3).reshape(row_tiles * BLOCK, col_tiles * BLOCK)


def matrix_to_tiles(matrix):
    row_tiles = matrix.shape[0] // BLOCK
    col_tiles = matrix.shape[1] // BLOCK
    blocked = matrix.reshape(row_tiles, BLOCK, col_tiles, BLOCK)
    return blocked.transpose(0, 2, 1, 3).reshape(row_tiles * col_tiles, BLOCK, BLOCK)


def exchange(values, axes):
    return lax.all_to_all(values, axes, split_axis=0, concat_axis=0, tiled=True)


def spread(values, axes):
    count = lax.axis_size(axes)
    return exchange(jnp.broadcast_to(values[None], (count,) + values.shape), axes)


def exchange_sum(values, axes):
    return jnp.sum(exchange(values, axes).astype(jnp.float32), axis=0)


def shard_owners(owner_slot, shard_count, shard_groups):
    padded = shard_count * shard_groups
    first = ATTN_TILES
    members = []
    for _ in range(2):
        grid = owner_slot[first : first + GRID_D * GRID_FF].reshape(GRID_D, GRID_FF)
        grid = jnp.pad(grid, ((0, 0), (0, padded - GRID_FF)), constant_values=-1)
        members.append(
            grid.reshape(GRID_D, shard_count, shard_groups).transpose(1, 0, 2).reshape(shard_count, -1)
        )
        first = first + GRID_D * GRID_FF
    grid = owner_slot[first : first + GRID_D * GRID_FF].reshape(GRID_FF, GRID_D)
    grid = jnp.pad(grid, ((0, padded - GRID_FF), (0, 0)), constant_values=-1)
    members.append(grid.reshape(shard_count, -1))
    return jnp.concatenate(members, axis=1)


def attention_owners(owner_slot, shard_count, shard_rows):
    grids = []
    first = 0
    for row_count, col_count in matrix_shapes()[:4]:
        tile_count = row_count // BLOCK * (col_count // BLOCK)
        grids.append(owner_slot[first : first + tile_count].reshape(row_count // BLOCK, -1))
        first = first + tile_count
    members = []
    for grid in (jnp.concatenate(grids[:3], axis=1), grids[3]):
        missing = shard_count * shard_rows - grid.shape[0]
        grid = jnp.pad(grid, ((0, missing), (0, 0)), constant_values=-1)
        members.append(grid.reshape(shard_count, -1))
    return jnp.concatenate(members, axis=1)


def split_columns(values, shard_count, shard_rows):
    width = shard_rows * BLOCK
    padded = jnp.pad(values, ((0, 0), (0, shard_count * width - values.shape[1])))
    parts = padded.reshape(values.shape[0], shard_count, width).transpose(1, 0, 2)
    return exchange(parts, "blk").reshape(-1, width)


class Route:
    def __init__(self, owners, slot_local, factors):
        uly_count = lax.axis_size("uly")
        blk_count = lax.axis_size("blk")
        blk_index = lax.axis_index("blk")
        self.column_count = lax.axis_size("dp") * uly_count
        self.column = lax.axis_index("dp") * uly_count + lax.axis_index("uly")
        self.device = (lax.axis_index("dp") * blk_count + blk_index) * uly_count + lax.axis_index(
            "uly"
        )
        self.tiles = owners.shape[1]
        self.pair_cap = capacity(self.tiles / (self.column_count * blk_count), factors[0], slot_local)
        self.column_cap = capacity(self.tiles / self.column_count, factors[1], self.tiles)
        flat = owners.reshape(-1)
        self.owner = flat
        self.first = self.device * slot_local
        self.real = flat >= 0
        self.shard = jnp.repeat(jnp.arange(blk_count, dtype=jnp.int32), self.tiles)
        self.holder = jnp.maximum(flat, 0) // slot_local
        columns = self.holder // (blk_count * uly_count) * uly_count + self.holder % uly_count
        source = self.holder // uly_count % blk_count
        self.pair_rank = earlier_equal(jnp.where(self.real, self.holder * blk_count + self.shard, -1))
        line_rank = earlier_equal(jnp.where(self.real, columns * blk_count + self.shard, -1))
        self.fits = (jnp.max(jnp.where(self.real, self.pair_rank, 0)) < self.pair_cap) & (
            jnp.max(jnp.where(self.real, line_rank, 0)) < self.column_cap
        )

        def mine(values):
            return lax.dynamic_slice_in_dim(values, blk_index * self.tiles, self.tiles, 0)

        self.my_owner = mine(flat)
        self.my_rank = mine(line_rank)
        my_real = mine(self.real)
        my_columns = mine(columns)
        my_pair_rank = mine(self.pair_rank)
        self.place = jnp.where(my_real, my_columns * self.column_cap + self.my_rank, -1)
        self.held = my_real & (my_columns == self.column) & (my_pair_rank < self.pair_cap)
        self.arrival = mine(source) * self.pair_cap + my_pair_rank
        self.pair_slots = jnp.arange(blk_count * self.pair_cap, dtype=jnp.int32)

    def slot_position(self):
        return self.shard * self.pair_cap + self.pair_rank

    def send_index(self):
        key = jnp.where(
            self.real & (self.holder == self.device) & (self.pair_rank < self.pair_cap),
            self.slot_position(),
            -1,
        )
        return locate(self.pair_slots, key, self.owner - self.first)

    def compact_index(self):
        wanted = jnp.arange(self.column_cap, dtype=jnp.int32)
        return locate(wanted, jnp.where(self.held, self.my_rank, -1), self.arrival)

    def send_home(self, tiles):
        wanted = jnp.arange(self.column_count * self.column_cap, dtype=jnp.int32)
        index = locate(wanted, self.place, jnp.arange(self.tiles, dtype=jnp.int32))
        summed = lax.psum_scatter(
            pick(tiles, index), COLUMN_AXES, scatter_dimension=0, tiled=True
        )
        back = locate(self.pair_slots, jnp.where(self.held, self.arrival, -1), self.my_rank)
        return exchange(pick(summed, back), "blk")


def rotate(values, positions, direction):
    half_size = HD // 2
    frequency = ROPE_BASE ** (-2.0 * jnp.arange(half_size, dtype=jnp.float32) / HD)
    angles = positions.astype(jnp.float32)[:, None] * frequency[None, :]
    cosine = jnp.cos(angles)[:, None, :]
    sine = direction * jnp.sin(angles)[:, None, :]
    first_half = values[..., :half_size]
    second_half = values[..., half_size:]
    return jnp.concatenate(
        [first_half * cosine - second_half * sine, second_half * cosine + first_half * sine],
        axis=-1,
    )


def forward_product(left_side, weight):
    return jnp.dot(left_side, weight, preferred_element_type=jnp.float32)


def back_product(grads, weight):
    return jnp.einsum("nf,df->nd", grads, weight, preferred_element_type=jnp.float32)


def outer_product(left_side, right_side):
    return jnp.einsum(
        "nb,nc->bc", left_side, right_side, preferred_element_type=jnp.float32
    ).astype(jnp.bfloat16)


def norm_backward(values, inverse, gain, grad_normed):
    scaled = values * inverse
    gained = grad_normed * gain
    grad_values = inverse * (gained - scaled * jnp.mean(gained * scaled, axis=-1, keepdims=True))
    return (grad_values, jnp.sum(grad_normed * scaled, axis=0))


def local(
    tokens,
    cotangent,
    lengths,
    owner_slot,
    master,
    moment_first,
    moment_second,
    basis_left,
    basis_right,
    small_master,
    small_first,
    small_second,
):
    uly_count = lax.axis_size("uly")
    blk_count = lax.axis_size("blk")
    all_count = lax.axis_size("dp") * blk_count * uly_count
    uly_index = lax.axis_index("uly")
    blk_index = lax.axis_index("blk")
    seq_count = tokens.shape[0]
    rows_local = tokens.shape[1]
    token_count = seq_count * rows_local
    span_rows = rows_local * uly_count
    heads_local = QH // uly_count
    slot_local = master.shape[0]
    slot_total = slot_local * all_count
    score_root = math.sqrt(HD)
    positions = (blk_index * uly_count + uly_index) * rows_local + jnp.arange(
        rows_local, dtype=jnp.int32
    )
    query_pos = blk_index * span_rows + jnp.arange(span_rows, dtype=jnp.int32)
    head_of = [member * heads_local // (QH // KVH) for member in range(uly_count)]
    shard_groups = -(-GRID_FF // blk_count)
    shard_rows = -(-GRID_D // blk_count)
    attn_cap = capacity(ATTN_TILES / all_count, 3.8, slot_local)
    route = Route(shard_owners(owner_slot, blk_count, shard_groups), slot_local, (3.5, 3.45))
    attn_route = Route(attention_owners(owner_slot, blk_count, shard_rows), slot_local, (5.0, 3.8))
    my_first = route.first
    attn_owner = owner_slot[:ATTN_TILES]
    attn_device = attn_owner // slot_local
    attn_rank = earlier_equal(attn_device)
    fits_attn = jnp.max(attn_rank) < attn_cap
    attn_send = locate(
        jnp.arange(attn_cap, dtype=jnp.int32),
        jnp.where(attn_device == route.device, attn_rank, -1),
        attn_owner - my_first,
    )
    attn_place = attn_device * attn_cap + attn_rank

    master_low = master.astype(jnp.bfloat16)
    small_copies = spread(small_master.astype(jnp.bfloat16), ALL_AXES).reshape(-1)
    attn_buffer = lax.all_gather(pick(master_low, attn_send), ALL_AXES, axis=0, tiled=True)

    def whole_tiles(index):
        return pick(lax.all_gather(master_low, ALL_AXES, axis=0, tiled=True), index)

    attn_tiles = lax.cond(
        fits_attn, lambda: pick(attn_buffer, attn_place), lambda: whole_tiles(attn_owner)
    )
    arrived_tiles = exchange(pick(master_low, route.send_index()), "blk")
    shard_buffer = lax.all_gather(
        pick(arrived_tiles, route.compact_index()), COLUMN_AXES, axis=0, tiled=True
    )
    shard_stack = lax.cond(
        route.fits, lambda: pick(shard_buffer, route.place), lambda: whole_tiles(route.my_owner)
    )
    third = GRID_D * shard_groups
    real_groups = (
        blk_index * shard_groups + jnp.arange(shard_groups, dtype=jnp.int32)
    ) < GRID_FF
    real_hidden = jnp.repeat(real_groups, BLOCK)
    w_gate = jnp.where(
        real_hidden[None, :], tiles_to_matrix(shard_stack[:third], GRID_D, shard_groups), 0
    )
    w_up = jnp.where(
        real_hidden[None, :], tiles_to_matrix(shard_stack[third : 2 * third], GRID_D, shard_groups), 0
    )
    w_down = jnp.where(
        real_hidden[:, None], tiles_to_matrix(shard_stack[2 * third :], shard_groups, GRID_D), 0
    )
    attn_matrices = []
    first = 0
    for row_count, col_count in matrix_shapes()[:4]:
        tile_count = row_count // BLOCK * (col_count // BLOCK)
        attn_matrices.append(
            tiles_to_matrix(
                attn_tiles[first : first + tile_count], row_count // BLOCK, col_count // BLOCK
            )
        )
        first = first + tile_count
    w_query, w_key, w_value, w_out = attn_matrices
    smalls = [member.astype(jnp.float32) for member in split_small(small_copies)]
    gain_first, gain_second, bias_query, bias_key, bias_value = smalls
    valid_rows = (positions[None, :] < lengths[:, None]).astype(jnp.float32)
    seed_grad = (cotangent.astype(jnp.float32) * valid_rows[:, :, None]).reshape(token_count, D)
    seed_low = seed_grad.astype(jnp.bfloat16)
    seed_line = spread(seed_low, "blk").reshape(blk_count * token_count, D)
    token_rows = tokens.reshape(token_count, D).astype(jnp.float32)
    inverse_first = lax.rsqrt(jnp.mean(token_rows * token_rows, axis=-1, keepdims=True) + NORM_EPS)
    normed = (token_rows * inverse_first * gain_first).astype(jnp.bfloat16)
    query_lin = forward_product(normed, w_query) + bias_query
    key_lin = forward_product(normed, w_key) + bias_key
    value_rows = (
        (forward_product(normed, w_value) + bias_value)
        .astype(jnp.bfloat16)
        .reshape(seq_count, rows_local, KVH, HD)
    )
    query_rot = rotate(query_lin.reshape(seq_count, rows_local, QH, HD), positions, 1.0).astype(
        jnp.bfloat16
    )
    key_rot = rotate(key_lin.reshape(seq_count, rows_local, KVH, HD), positions, 1.0).astype(
        jnp.bfloat16
    )
    query_heads = lax.all_to_all(query_rot, "uly", split_axis=2, concat_axis=1, tiled=True)
    key_value = jnp.concatenate([key_rot, value_rows], axis=-1)
    key_value = jnp.stack([key_value[:, :, head] for head in head_of], axis=0)
    key_value = exchange(key_value, "uly").transpose(1, 0, 2, 3)
    key_value = spread(key_value, "blk").transpose(1, 0, 2, 3, 4)
    key_value = key_value.reshape(seq_count, blk_count * span_rows, 2 * HD)
    keys = key_value[..., :HD]
    values = key_value[..., HD:]
    key_pos = jnp.arange(blk_count * span_rows, dtype=jnp.int32)
    allowed = (key_pos[None, None, :] <= query_pos[None, :, None]) & (
        key_pos[None, None, :] < lengths[:, None, None]
    )
    allowed = allowed[:, :, None, :]
    scores = (
        jnp.einsum("sqhd,skd->sqhk", query_heads, keys, preferred_element_type=jnp.float32)
        / score_root
    )
    scores = jnp.where(allowed, scores, MASK_FILL)
    top = jnp.max(scores, axis=-1, keepdims=True)
    weights = jnp.where(allowed, jnp.exp(scores - top), 0.0)
    probs = weights / jnp.sum(weights, axis=-1, keepdims=True)
    probs_low = probs.astype(jnp.bfloat16)
    attended = jnp.einsum(
        "sqhk,skd->sqhd", probs_low, values, preferred_element_type=jnp.float32
    )
    out_rows = lax.all_to_all(
        attended.astype(jnp.bfloat16), "uly", split_axis=1, concat_axis=2, tiled=True
    ).reshape(token_count, QW)
    middle = token_rows + forward_product(out_rows, w_out)
    inverse_second = lax.rsqrt(jnp.mean(middle * middle, axis=-1, keepdims=True) + NORM_EPS)
    normed_two = (middle * inverse_second * gain_second).astype(jnp.bfloat16)
    normed_line = spread(normed_two, "blk").reshape(blk_count * token_count, D)
    gate_lin = forward_product(normed_line, w_gate)
    upward = forward_product(normed_line, w_up)
    hidden = (jax.nn.silu(gate_lin) * upward).astype(jnp.bfloat16)
    grad_hidden = back_product(seed_line, w_down)
    gate_sigmoid = jax.nn.sigmoid(gate_lin)
    grad_gate = (
        grad_hidden * upward * gate_sigmoid * (1.0 + gate_lin * (1.0 - gate_sigmoid))
    ).astype(jnp.bfloat16)
    grad_up = (grad_hidden * gate_lin * gate_sigmoid).astype(jnp.bfloat16)
    grad_line = back_product(grad_gate, w_gate) + back_product(grad_up, w_up)
    grad_normed_two = exchange_sum(
        grad_line.astype(jnp.bfloat16).reshape(blk_count, token_count, D), "blk"
    )
    mixed_line = forward_product(hidden, w_down).astype(jnp.bfloat16)
    mixed_out = (
        (middle + exchange_sum(mixed_line.reshape(blk_count, token_count, D), "blk"))
        .astype(jnp.bfloat16)
        .reshape(seq_count, rows_local, D)
    )
    shard_grads = jnp.concatenate(
        [
            matrix_to_tiles(outer_product(normed_line, grad_gate)),
            matrix_to_tiles(outer_product(normed_line, grad_up)),
            matrix_to_tiles(outer_product(hidden, seed_line)),
        ],
        axis=0,
    )
    returned_grads = route.send_home(shard_grads)
    norm_part_two, gain_second_grad = norm_backward(
        middle, inverse_second, gain_second, grad_normed_two
    )
    grad_middle = seed_grad + norm_part_two
    grad_middle_low = grad_middle.astype(jnp.bfloat16)
    grad_out_rows = (
        back_product(grad_middle_low, w_out)
        .astype(jnp.bfloat16)
        .reshape(seq_count, rows_local, QH, HD)
    )
    grad_heads = lax.all_to_all(grad_out_rows, "uly", split_axis=2, concat_axis=1, tiled=True)
    grad_heads_wide = grad_heads.astype(jnp.float32)
    row_delta = jnp.sum(grad_heads_wide * attended, axis=-1)

    grad_prob = jnp.einsum(
        "sqhd,skd->sqhk", grad_heads, values, preferred_element_type=jnp.float32
    )
    grad_score = (probs * (grad_prob - row_delta[..., None])).astype(jnp.bfloat16)
    grad_query = jnp.einsum(
        "sqhk,skd->sqhd", grad_score, keys, preferred_element_type=jnp.float32
    )
    grad_keys = jnp.einsum(
        "sqhk,sqhd->skd", grad_score, query_heads, preferred_element_type=jnp.float32
    )
    grad_values = jnp.einsum(
        "sqhk,sqhd->skd", probs_low, grad_heads, preferred_element_type=jnp.float32
    )
    grad_query_low = (grad_query / score_root).astype(jnp.bfloat16)
    grad_query_rows = lax.all_to_all(grad_query_low, "uly", split_axis=1, concat_axis=2, tiled=True)
    grad_pair = jnp.concatenate([grad_keys / score_root, grad_values], axis=-1).astype(jnp.bfloat16)
    grad_pair = grad_pair.reshape(seq_count, blk_count, span_rows, 2 * HD).transpose(1, 0, 2, 3)
    grad_pair = exchange_sum(grad_pair, "blk").astype(jnp.bfloat16)
    grad_pair = grad_pair.reshape(seq_count, uly_count, rows_local, 2 * HD).transpose(1, 0, 2, 3)
    grad_pair = exchange(grad_pair, "uly").astype(jnp.float32)
    grad_pair = jnp.stack(
        [
            sum(grad_pair[member] for member in range(uly_count) if head_of[member] == head)
            for head in range(KVH)
        ],
        axis=2,
    )
    grad_keys_rows = grad_pair[..., :HD]
    grad_values_rows = grad_pair[..., HD:]
    grad_query_lin = (
        rotate(grad_query_rows.astype(jnp.float32), positions, -1.0)
        .astype(jnp.bfloat16)
        .reshape(token_count, QW)
    )
    key_rounded = grad_keys_rows
    grad_key_lin = (
        rotate(key_rounded, positions, -1.0).astype(jnp.bfloat16).reshape(token_count, KVW)
    )
    grad_value_lin = grad_values_rows.astype(jnp.bfloat16).reshape(token_count, KVW)
    grad_normed = (
        back_product(grad_query_lin, w_query)
        + back_product(grad_key_lin, w_key)
        + back_product(grad_value_lin, w_value)
    )
    norm_part_first, gain_first_grad = norm_backward(
        token_rows, inverse_first, gain_first, grad_normed
    )
    grad_tokens = (grad_middle + norm_part_first).reshape(seq_count, rows_local, D)
    small_partial = jnp.concatenate(
        [
            gain_first_grad,
            gain_second_grad,
            jnp.sum(grad_query_lin, axis=0, dtype=jnp.float32),
            jnp.sum(grad_key_lin, axis=0, dtype=jnp.float32),
            jnp.sum(grad_value_lin, axis=0, dtype=jnp.float32),
        ]
    )
    grad_small = exchange_sum(small_partial.reshape(all_count, -1), ALL_AXES)
    grad_lines = spread(
        jnp.concatenate([grad_query_lin, grad_key_lin, grad_value_lin], axis=1), "blk"
    ).reshape(blk_count * token_count, QW + 2 * KVW)
    middle_lines = spread(grad_middle_low, "blk").reshape(blk_count * token_count, D)
    attn_grads = jnp.concatenate(
        [
            matrix_to_tiles(
                outer_product(split_columns(normed, blk_count, shard_rows), grad_lines)
            ),
            matrix_to_tiles(
                outer_product(split_columns(out_rows, blk_count, shard_rows), middle_lines)
            ),
        ],
        axis=0,
    )
    attn_returned = attn_route.send_home(attn_grads)
    my_slots = my_first + jnp.arange(slot_local, dtype=jnp.int32)
    slot_index = locate(my_slots, route.owner, route.slot_position()) + locate(
        my_slots, attn_route.owner, blk_count * route.pair_cap + attn_route.slot_position()
    )
    slot_used = jnp.any(my_slots[:, None] == owner_slot[None, :], axis=1)

    def routed_grads():
        return pick(jnp.concatenate([returned_grads, attn_returned], axis=0), slot_index)

    def summed_grads():
        every_slot = jnp.arange(slot_total, dtype=jnp.int32)
        tile_owner = jnp.concatenate([route.my_owner, attn_route.my_owner])
        index = locate(every_slot, tile_owner, jnp.arange(tile_owner.shape[0], dtype=jnp.int32))
        held = jnp.any(every_slot[:, None] == tile_owner[None, :], axis=1)
        parts = pick(jnp.concatenate([shard_grads, attn_grads], axis=0), index)
        parts = jnp.where(held[:, None, None], parts, 0)
        return lax.psum_scatter(parts, ALL_AXES, scatter_dimension=0, tiled=True)

    grad_slots = lax.cond(route.fits & attn_route.fits, routed_grads, summed_grads)
    grad_slots = jnp.where(slot_used[:, None, None], grad_slots, 0).astype(jnp.float32)
    rotated = jnp.einsum("sji,sjk->sik", basis_left, grad_slots, precision=TOP_PRECISION)
    rotated = jnp.einsum("sik,skl->sil", rotated, basis_right, precision=TOP_PRECISION)
    first_new = BETA_FIRST * moment_first + (1.0 - BETA_FIRST) * rotated
    second_new = BETA_SECOND * moment_second + (1.0 - BETA_SECOND) * rotated * rotated
    normalized = first_new / (jnp.sqrt(second_new) + ADAM_EPS)
    update = jnp.einsum("sik,skl->sil", basis_left, normalized, precision=TOP_PRECISION)
    update = jnp.einsum("sik,slk->sil", update, basis_right, precision=TOP_PRECISION)
    tile_scale = jnp.sqrt(jnp.mean(master * master, axis=(1, 2), keepdims=True) + SCALE_EPS)
    master_new = master - RELATIVE_RATE * tile_scale * (update + WEIGHT_DECAY * master)
    small_first_new = BETA_FIRST * small_first + (1.0 - BETA_FIRST) * grad_small
    small_second_new = BETA_SECOND * small_second + (1.0 - BETA_SECOND) * grad_small * grad_small
    small_new = small_master - SMALL_RATE * (
        small_first_new / (jnp.sqrt(small_second_new) + ADAM_EPS) + WEIGHT_DECAY * small_master
    )
    return (
        mixed_out,
        grad_tokens,
        first_new,
        second_new,
        master_new,
        small_first_new,
        small_second_new,
        small_new,
    )


def solution(mesh):
    in_specs = (
        P("dp", ("blk", "uly"), None),
        P("dp", ("blk", "uly"), None),
        P("dp"),
        P(),
        P(("dp", "blk", "uly"), None, None),
        P(("dp", "blk", "uly"), None, None),
        P(("dp", "blk", "uly"), None, None),
        P(("dp", "blk", "uly"), None, None),
        P(("dp", "blk", "uly"), None, None),
        P(("dp", "blk", "uly")),
        P(("dp", "blk", "uly")),
        P(("dp", "blk", "uly")),
    )
    out_specs = (
        P("dp", ("blk", "uly"), None),
        P("dp", ("blk", "uly"), None),
        P(("dp", "blk", "uly"), None, None),
        P(("dp", "blk", "uly"), None, None),
        P(("dp", "blk", "uly"), None, None),
        P(("dp", "blk", "uly")),
        P(("dp", "blk", "uly")),
        P(("dp", "blk", "uly")),
    )
    return jax.shard_map(local, mesh=mesh, in_specs=in_specs, out_specs=out_specs, check_vma=False)
```

```python
import math

import jax
import jax.numpy as jnp
import numpy as np
from jax import lax
from jax.experimental import pallas as pl
from jax.experimental.pallas import tpu as pltpu
from jax.sharding import PartitionSpec as P

D = 1536
QH = 12
KVH = 2
HD = 128
FF = 8960
BLOCK = 128
QW = 1536
KVW = 256


NORM_EPS = 1e-06
ROPE_BASE = 1000000.0
BETA_FIRST = 0.5
BETA_SECOND = 0.5
ADAM_EPS = 1e-08
SCALE_EPS = 1e-06
RELATIVE_RATE = 0.5
SMALL_RATE = 0.25
WEIGHT_DECAY = 0.01
MASK_FILL = -1e30
TOP_PRECISION = lax.Precision.DEFAULT


def matrix_shapes():
    return [(D, QW), (D, KVW), (D, KVW), (QW, D), (D, FF), (D, FF), (FF, D)]


def split_small(vector):
    edges = [0, D, 2 * D, 2 * D + QW, 2 * D + QW + KVW, 2 * D + QW + 2 * KVW]
    return [vector[edges[number] : edges[number + 1]] for number in range(5)]


GRID_D = D // BLOCK
GRID_FF = FF // BLOCK
ATTN_TILES = GRID_D * (QW + 2 * KVW) // BLOCK + QW // BLOCK * GRID_D
ALL_AXES = ("dp", "blk", "uly")
COLUMN_AXES = ("dp", "uly")


def capacity(mean, factor, limit):
    return int(min(limit, math.ceil(mean + factor * math.sqrt(mean))))


def pick(table, index):
    return jnp.take(table, index, axis=0, mode="clip")


def earlier_equal(keys):
    number = jnp.arange(keys.shape[0], dtype=jnp.int32)
    same = keys[None, :] == keys[:, None]
    return jnp.sum((same & (number[None, :] < number[:, None])).astype(jnp.int32), axis=1)


def locate(wanted, keys, values):
    return jnp.sum(jnp.where(wanted[:, None] == keys[None, :], values[None, :], 0), axis=1)


def tiles_to_matrix(tiles, row_tiles, col_tiles):
    blocked = tiles.reshape(row_tiles, col_tiles, BLOCK, BLOCK)
    return blocked.transpose(0, 2, 1, 3).reshape(row_tiles * BLOCK, col_tiles * BLOCK)


def matrix_to_tiles(matrix):
    row_tiles = matrix.shape[0] // BLOCK
    col_tiles = matrix.shape[1] // BLOCK
    blocked = matrix.reshape(row_tiles, BLOCK, col_tiles, BLOCK)
    return blocked.transpose(0, 2, 1, 3).reshape(row_tiles * col_tiles, BLOCK, BLOCK)


def exchange(values, axes):
    return lax.all_to_all(values, axes, split_axis=0, concat_axis=0, tiled=True)


def spread(values, axes):
    count = lax.axis_size(axes)
    return exchange(jnp.broadcast_to(values[None], (count,) + values.shape), axes)


def exchange_sum(values, axes):
    return jnp.sum(exchange(values, axes).astype(jnp.float32), axis=0)


STEP_GROUPS = 2
STEP_TILES = 3 * STEP_GROUPS * GRID_D
STEP_COLUMNS = STEP_GROUPS * BLOCK
ROW_CHUNK = 512


def shard_owners(owner_slot, shard_count, shard_groups):
    missing = shard_count * shard_groups - GRID_FF
    first = ATTN_TILES
    members = []
    for number in range(3):
        grid = owner_slot[first : first + GRID_D * GRID_FF]
        if number < 2:
            grid = grid.reshape(GRID_D, GRID_FF).transpose(1, 0)
        else:
            grid = grid.reshape(GRID_FF, GRID_D)
        grid = jnp.pad(grid, ((0, missing), (0, 0)), constant_values=-1)
        members.append(
            grid.reshape(shard_count, shard_groups // STEP_GROUPS, STEP_GROUPS * GRID_D)
        )
        first = first + GRID_D * GRID_FF
    return jnp.stack(members, axis=2).reshape(shard_count, -1)


def mix_kernel(first_ref, x_ref, xt_ref, seed_ref, w_ref, tiles_ref, grad_ref, mixed_ref, acc_grad, acc_mixed):
    step = pl.program_id(0)
    kind = STEP_GROUPS * GRID_D

    @pl.when(step == 0)
    def _():
        acc_grad[...] = jnp.zeros_like(acc_grad)
        acc_mixed[...] = jnp.zeros_like(acc_mixed)

    def tall(first):
        return jnp.concatenate(
            [
                w_ref[first + group * GRID_D : first + (group + 1) * GRID_D].reshape(D, BLOCK)
                for group in range(STEP_GROUPS)
            ],
            axis=1,
        )

    def product(left, right, dims):
        return lax.dot_general(left, right, (dims, ((), ())), preferred_element_type=jnp.float32)

    w_gate = tall(0)
    w_up = tall(kind)
    w_down = jnp.concatenate(
        [
            jnp.concatenate(
                [w_ref[2 * kind + group * GRID_D + col] for col in range(GRID_D)], axis=1
            )
            for group in range(STEP_GROUPS)
        ],
        axis=0,
    )
    rows = x_ref.shape[0]
    real_columns = (GRID_FF - first_ref[0] - step * STEP_GROUPS) * BLOCK
    real = lax.broadcasted_iota(jnp.int32, (rows, STEP_COLUMNS), 1) < real_columns
    x = x_ref[...]
    seed = seed_ref[...]
    gate = product(x, w_gate, ((1,), (0,)))
    upward = product(x, w_up, ((1,), (0,)))
    grad_hidden = product(seed, w_down, ((1,), (1,)))
    sig = 1.0 / (1.0 + jnp.exp(-gate))
    silu = gate * sig
    hidden = jnp.where(real, silu * upward, 0.0).astype(jnp.bfloat16)
    grad_gate = jnp.where(
        real, grad_hidden * upward * sig * (1.0 + gate * (1.0 - sig)), 0.0
    ).astype(jnp.bfloat16)
    grad_up = jnp.where(real, grad_hidden * silu, 0.0).astype(jnp.bfloat16)
    acc_grad[...] += product(grad_gate, w_gate, ((1,), (1,))) + product(
        grad_up, w_up, ((1,), (1,))
    )
    acc_mixed[...] += product(hidden, w_down, ((1,), (0,)))
    xt = xt_ref[...]
    for number, right in ((0, grad_gate), (1, grad_up)):
        part = product(xt, right, ((1,), (0,))).astype(jnp.bfloat16)
        for group in range(STEP_GROUPS):
            first = number * kind + group * GRID_D
            tiles_ref[first : first + GRID_D] = part[
                :, group * BLOCK : (group + 1) * BLOCK
            ].reshape(GRID_D, BLOCK, BLOCK)
    part = product(hidden, seed, ((0,), (0,))).astype(jnp.bfloat16)
    for group in range(STEP_GROUPS):
        for col in range(GRID_D):
            tiles_ref[2 * kind + group * GRID_D + col] = part[
                group * BLOCK : (group + 1) * BLOCK, col * BLOCK : (col + 1) * BLOCK
            ]

    @pl.when(step == pl.num_programs(0) - 1)
    def _():
        grad_ref[...] = acc_grad[...].astype(grad_ref.dtype)
        mixed_ref[...] = acc_mixed[...].astype(mixed_ref.dtype)


def mix_chunk(first_group, x, seed, stack):
    rows = x.shape[0]
    steps = stack.shape[0] // STEP_TILES

    def fixed(shape):
        return pl.BlockSpec(shape, lambda step, first: (0,) * len(shape))

    tiles = pl.BlockSpec((STEP_TILES, BLOCK, BLOCK), lambda step, first: (step, 0, 0))
    return pl.pallas_call(
        mix_kernel,
        out_shape=(
            jax.ShapeDtypeStruct(stack.shape, jnp.bfloat16),
            jax.ShapeDtypeStruct((rows, D), jnp.bfloat16),
            jax.ShapeDtypeStruct((rows, D), jnp.bfloat16),
        ),
        grid_spec=pltpu.PrefetchScalarGridSpec(
            num_scalar_prefetch=1,
            grid=(steps,),
            in_specs=[fixed((rows, D)), fixed((D, rows)), fixed((rows, D)), tiles],
            out_specs=(tiles, fixed((rows, D)), fixed((rows, D))),
            scratch_shapes=[pltpu.VMEM((rows, D), jnp.float32), pltpu.VMEM((rows, D), jnp.float32)],
        ),
        compiler_params=pltpu.CompilerParams(
            dimension_semantics=("arbitrary",), vmem_limit_bytes=56 * 1024 * 1024
        ),
    )(first_group, x, x.T, seed, stack)


def mix_lines(first_group, x, seed, stack):
    parts = []
    for first in range(0, x.shape[0], ROW_CHUNK):
        last = min(first + ROW_CHUNK, x.shape[0])
        parts.append(mix_chunk(first_group, x[first:last], seed[first:last], stack))
    if len(parts) == 1:
        return parts[0]
    tiles = sum(part[0].astype(jnp.float32) for part in parts).astype(jnp.bfloat16)
    return (
        tiles,
        jnp.concatenate([part[1] for part in parts], axis=0),
        jnp.concatenate([part[2] for part in parts], axis=0),
    )


def attention_owners(owner_slot, shard_count, shard_rows):
    grids = []
    first = 0
    for row_count, col_count in matrix_shapes()[:4]:
        tile_count = row_count // BLOCK * (col_count // BLOCK)
        grids.append(owner_slot[first : first + tile_count].reshape(row_count // BLOCK, -1))
        first = first + tile_count
    members = []
    for grid in (jnp.concatenate(grids[:3], axis=1), grids[3]):
        missing = shard_count * shard_rows - grid.shape[0]
        grid = jnp.pad(grid, ((0, missing), (0, 0)), constant_values=-1)
        members.append(grid.reshape(shard_count, -1))
    return jnp.concatenate(members, axis=1)


def split_columns(values, shard_count, shard_rows):
    width = shard_rows * BLOCK
    padded = jnp.pad(values, ((0, 0), (0, shard_count * width - values.shape[1])))
    parts = padded.reshape(values.shape[0], shard_count, width).transpose(1, 0, 2)
    return exchange(parts, "blk").reshape(-1, width)


class Route:
    def __init__(self, owners, slot_local, factors):
        uly_count = lax.axis_size("uly")
        blk_count = lax.axis_size("blk")
        blk_index = lax.axis_index("blk")
        self.column_count = lax.axis_size("dp") * uly_count
        self.column = lax.axis_index("dp") * uly_count + lax.axis_index("uly")
        self.device = (lax.axis_index("dp") * blk_count + blk_index) * uly_count + lax.axis_index(
            "uly"
        )
        self.tiles = owners.shape[1]
        self.pair_cap = capacity(self.tiles / (self.column_count * blk_count), factors[0], slot_local)
        self.column_cap = capacity(self.tiles / self.column_count, factors[1], self.tiles)
        flat = owners.reshape(-1)
        self.owner = flat
        self.first = self.device * slot_local
        self.real = flat >= 0
        self.shard = jnp.repeat(jnp.arange(blk_count, dtype=jnp.int32), self.tiles)
        self.holder = jnp.maximum(flat, 0) // slot_local
        columns = self.holder // (blk_count * uly_count) * uly_count + self.holder % uly_count
        source = self.holder // uly_count % blk_count
        self.pair_rank = earlier_equal(jnp.where(self.real, self.holder * blk_count + self.shard, -1))
        line_rank = earlier_equal(jnp.where(self.real, columns * blk_count + self.shard, -1))
        self.fits = (jnp.max(jnp.where(self.real, self.pair_rank, 0)) < self.pair_cap) & (
            jnp.max(jnp.where(self.real, line_rank, 0)) < self.column_cap
        )

        def mine(values):
            return lax.dynamic_slice_in_dim(values, blk_index * self.tiles, self.tiles, 0)

        self.my_owner = mine(flat)
        self.my_rank = mine(line_rank)
        my_real = mine(self.real)
        my_columns = mine(columns)
        my_pair_rank = mine(self.pair_rank)
        self.place = jnp.where(my_real, my_columns * self.column_cap + self.my_rank, -1)
        self.held = my_real & (my_columns == self.column) & (my_pair_rank < self.pair_cap)
        self.arrival = mine(source) * self.pair_cap + my_pair_rank
        self.pair_slots = jnp.arange(blk_count * self.pair_cap, dtype=jnp.int32)

    def slot_position(self):
        return self.shard * self.pair_cap + self.pair_rank

    def send_index(self):
        key = jnp.where(
            self.real & (self.holder == self.device) & (self.pair_rank < self.pair_cap),
            self.slot_position(),
            -1,
        )
        return locate(self.pair_slots, key, self.owner - self.first)

    def compact_index(self):
        wanted = jnp.arange(self.column_cap, dtype=jnp.int32)
        return locate(wanted, jnp.where(self.held, self.my_rank, -1), self.arrival)

    def home_buffer(self, tiles):
        wanted = jnp.arange(self.column_count * self.column_cap, dtype=jnp.int32)
        index = locate(wanted, self.place, jnp.arange(self.tiles, dtype=jnp.int32))
        return pick(tiles, index)

    def send_home(self, buffer):
        summed = lax.psum_scatter(buffer, COLUMN_AXES, scatter_dimension=0, tiled=True)
        back = locate(self.pair_slots, jnp.where(self.held, self.arrival, -1), self.my_rank)
        return exchange(pick(summed, back), "blk")


def rotate(values, positions, direction):
    half_size = HD // 2
    frequency = ROPE_BASE ** (-2.0 * jnp.arange(half_size, dtype=jnp.float32) / HD)
    angles = positions.astype(jnp.float32)[:, None] * frequency[None, :]
    cosine = jnp.cos(angles)[:, None, :]
    sine = direction * jnp.sin(angles)[:, None, :]
    first_half = values[..., :half_size]
    second_half = values[..., half_size:]
    return jnp.concatenate(
        [first_half * cosine - second_half * sine, second_half * cosine + first_half * sine],
        axis=-1,
    )


def forward_product(left_side, weight):
    return jnp.dot(left_side, weight, preferred_element_type=jnp.float32)


def back_product(grads, weight):
    return jnp.einsum("nf,df->nd", grads, weight, preferred_element_type=jnp.float32)


def outer_product(left_side, right_side):
    return jnp.einsum(
        "nb,nc->bc", left_side, right_side, preferred_element_type=jnp.float32
    ).astype(jnp.bfloat16)


def norm_backward(values, inverse, gain, grad_normed):
    scaled = values * inverse
    gained = grad_normed * gain
    grad_values = inverse * (gained - scaled * jnp.mean(gained * scaled, axis=-1, keepdims=True))
    return (grad_values, jnp.sum(grad_normed * scaled, axis=0))


def local(
    tokens,
    cotangent,
    lengths,
    owner_slot,
    master,
    moment_first,
    moment_second,
    basis_left,
    basis_right,
    small_master,
    small_first,
    small_second,
):
    uly_count = lax.axis_size("uly")
    blk_count = lax.axis_size("blk")
    all_count = lax.axis_size("dp") * blk_count * uly_count
    uly_index = lax.axis_index("uly")
    blk_index = lax.axis_index("blk")
    seq_count = tokens.shape[0]
    rows_local = tokens.shape[1]
    token_count = seq_count * rows_local
    span_rows = rows_local * uly_count
    heads_local = QH // uly_count
    slot_local = master.shape[0]
    slot_total = slot_local * all_count
    score_root = math.sqrt(HD)
    positions = (blk_index * uly_count + uly_index) * rows_local + jnp.arange(
        rows_local, dtype=jnp.int32
    )
    query_pos = blk_index * span_rows + jnp.arange(span_rows, dtype=jnp.int32)
    head_of = [member * heads_local // (QH // KVH) for member in range(uly_count)]
    shard_groups = -(-GRID_FF // (blk_count * STEP_GROUPS)) * STEP_GROUPS
    shard_rows = -(-GRID_D // blk_count)
    attn_cap = capacity(ATTN_TILES / all_count, 3.8, slot_local)
    route = Route(shard_owners(owner_slot, blk_count, shard_groups), slot_local, (3.5, 3.45))
    attn_route = Route(attention_owners(owner_slot, blk_count, shard_rows), slot_local, (5.0, 3.8))
    my_first = route.first
    attn_owner = owner_slot[:ATTN_TILES]
    attn_device = attn_owner // slot_local
    attn_rank = earlier_equal(attn_device)
    fits_attn = jnp.max(attn_rank) < attn_cap
    attn_send = locate(
        jnp.arange(attn_cap, dtype=jnp.int32),
        jnp.where(attn_device == route.device, attn_rank, -1),
        attn_owner - my_first,
    )
    attn_place = attn_device * attn_cap + attn_rank

    master_low = master.astype(jnp.bfloat16)
    small_copies = spread(small_master.astype(jnp.bfloat16), ALL_AXES).reshape(-1)
    attn_buffer = lax.all_gather(pick(master_low, attn_send), ALL_AXES, axis=0, tiled=True)

    def whole_tiles(index):
        return pick(lax.all_gather(master_low, ALL_AXES, axis=0, tiled=True), index)

    attn_tiles = lax.cond(
        fits_attn, lambda: pick(attn_buffer, attn_place), lambda: whole_tiles(attn_owner)
    )
    arrived_tiles = exchange(pick(master_low, route.send_index()), "blk")
    shard_buffer = lax.all_gather(
        pick(arrived_tiles, route.compact_index()), COLUMN_AXES, axis=0, tiled=True
    )
    shard_stack = lax.cond(
        route.fits, lambda: pick(shard_buffer, route.place), lambda: whole_tiles(route.my_owner)
    )
    attn_matrices = []
    first = 0
    for row_count, col_count in matrix_shapes()[:4]:
        tile_count = row_count // BLOCK * (col_count // BLOCK)
        attn_matrices.append(
            tiles_to_matrix(
                attn_tiles[first : first + tile_count], row_count // BLOCK, col_count // BLOCK
            )
        )
        first = first + tile_count
    w_query, w_key, w_value, w_out = attn_matrices
    smalls = [member.astype(jnp.float32) for member in split_small(small_copies)]
    gain_first, gain_second, bias_query, bias_key, bias_value = smalls
    valid_rows = (positions[None, :] < lengths[:, None]).astype(jnp.float32)
    seed_grad = (cotangent.astype(jnp.float32) * valid_rows[:, :, None]).reshape(token_count, D)
    seed_low = seed_grad.astype(jnp.bfloat16)
    seed_line = spread(seed_low, "blk").reshape(blk_count * token_count, D)
    token_rows = tokens.reshape(token_count, D).astype(jnp.float32)
    inverse_first = lax.rsqrt(jnp.mean(token_rows * token_rows, axis=-1, keepdims=True) + NORM_EPS)
    normed = (token_rows * inverse_first * gain_first).astype(jnp.bfloat16)
    query_lin = forward_product(normed, w_query) + bias_query
    key_lin = forward_product(normed, w_key) + bias_key
    value_rows = (
        (forward_product(normed, w_value) + bias_value)
        .astype(jnp.bfloat16)
        .reshape(seq_count, rows_local, KVH, HD)
    )
    query_rot = rotate(query_lin.reshape(seq_count, rows_local, QH, HD), positions, 1.0).astype(
        jnp.bfloat16
    )
    key_rot = rotate(key_lin.reshape(seq_count, rows_local, KVH, HD), positions, 1.0).astype(
        jnp.bfloat16
    )
    query_heads = lax.all_to_all(query_rot, "uly", split_axis=2, concat_axis=1, tiled=True)
    key_value = jnp.concatenate([key_rot, value_rows], axis=-1)
    key_value = jnp.stack([key_value[:, :, head] for head in head_of], axis=0)
    key_value = exchange(key_value, "uly").transpose(1, 0, 2, 3)
    key_value = spread(key_value, "blk").transpose(1, 0, 2, 3, 4)
    key_value = key_value.reshape(seq_count, blk_count * span_rows, 2 * HD)
    keys = key_value[..., :HD]
    values = key_value[..., HD:]
    key_pos = jnp.arange(blk_count * span_rows, dtype=jnp.int32)
    allowed = (key_pos[None, None, :] <= query_pos[None, :, None]) & (
        key_pos[None, None, :] < lengths[:, None, None]
    )
    allowed = allowed[:, :, None, :]
    scores = (
        jnp.einsum("sqhd,skd->sqhk", query_heads, keys, preferred_element_type=jnp.float32)
        / score_root
    )
    scores = jnp.where(allowed, scores, MASK_FILL)
    top = jnp.max(scores, axis=-1, keepdims=True)
    weights = jnp.where(allowed, jnp.exp(scores - top), 0.0)
    probs = weights / jnp.sum(weights, axis=-1, keepdims=True)
    probs_low = probs.astype(jnp.bfloat16)
    attended = jnp.einsum(
        "sqhk,skd->sqhd", probs_low, values, preferred_element_type=jnp.float32
    )
    out_rows = lax.all_to_all(
        attended.astype(jnp.bfloat16), "uly", split_axis=1, concat_axis=2, tiled=True
    ).reshape(token_count, QW)
    middle = token_rows + forward_product(out_rows, w_out)
    inverse_second = lax.rsqrt(jnp.mean(middle * middle, axis=-1, keepdims=True) + NORM_EPS)
    normed_two = (middle * inverse_second * gain_second).astype(jnp.bfloat16)
    normed_line = spread(normed_two, "blk").reshape(blk_count * token_count, D)
    first_group = jnp.full((1,), blk_index * shard_groups, jnp.int32)
    shard_grads, grad_line, mixed_line = mix_lines(
        first_group, normed_line, seed_line, shard_stack
    )
    grad_normed_two = exchange_sum(grad_line.reshape(blk_count, token_count, D), "blk")
    home_buffer = route.home_buffer(shard_grads)
    grad_normed_two, home_buffer = lax.optimization_barrier((grad_normed_two, home_buffer))
    returned_grads = route.send_home(home_buffer)
    norm_part_two, gain_second_grad = norm_backward(
        middle, inverse_second, gain_second, grad_normed_two
    )
    grad_middle = seed_grad + norm_part_two
    grad_middle_low = grad_middle.astype(jnp.bfloat16)
    grad_out_rows = (
        back_product(grad_middle_low, w_out)
        .astype(jnp.bfloat16)
        .reshape(seq_count, rows_local, QH, HD)
    )
    grad_heads = lax.all_to_all(grad_out_rows, "uly", split_axis=2, concat_axis=1, tiled=True)
    mixed_line, grad_heads = lax.optimization_barrier((mixed_line, grad_heads))
    mixed_out = (
        (middle + exchange_sum(mixed_line.reshape(blk_count, token_count, D), "blk"))
        .astype(jnp.bfloat16)
        .reshape(seq_count, rows_local, D)
    )
    grad_heads_wide = grad_heads.astype(jnp.float32)
    row_delta = jnp.sum(grad_heads_wide * attended, axis=-1)

    grad_prob = jnp.einsum(
        "sqhd,skd->sqhk", grad_heads, values, preferred_element_type=jnp.float32
    )
    grad_score = (probs * (grad_prob - row_delta[..., None])).astype(jnp.bfloat16)
    grad_query = jnp.einsum(
        "sqhk,skd->sqhd", grad_score, keys, preferred_element_type=jnp.float32
    )
    grad_keys = jnp.einsum(
        "sqhk,sqhd->skd", grad_score, query_heads, preferred_element_type=jnp.float32
    )
    grad_values = jnp.einsum(
        "sqhk,sqhd->skd", probs_low, grad_heads, preferred_element_type=jnp.float32
    )
    grad_query_low = (grad_query / score_root).astype(jnp.bfloat16)
    grad_query_rows = lax.all_to_all(grad_query_low, "uly", split_axis=1, concat_axis=2, tiled=True)
    grad_pair = jnp.concatenate([grad_keys / score_root, grad_values], axis=-1).astype(jnp.bfloat16)
    grad_pair = grad_pair.reshape(seq_count, blk_count, span_rows, 2 * HD).transpose(1, 0, 2, 3)
    grad_pair = exchange_sum(grad_pair, "blk").astype(jnp.bfloat16)
    grad_pair = grad_pair.reshape(seq_count, uly_count, rows_local, 2 * HD).transpose(1, 0, 2, 3)
    grad_pair = exchange(grad_pair, "uly").astype(jnp.float32)
    grad_pair = jnp.stack(
        [
            sum(grad_pair[member] for member in range(uly_count) if head_of[member] == head)
            for head in range(KVH)
        ],
        axis=2,
    )
    grad_keys_rows = grad_pair[..., :HD]
    grad_values_rows = grad_pair[..., HD:]
    grad_query_lin = (
        rotate(grad_query_rows.astype(jnp.float32), positions, -1.0)
        .astype(jnp.bfloat16)
        .reshape(token_count, QW)
    )
    key_rounded = grad_keys_rows
    grad_key_lin = (
        rotate(key_rounded, positions, -1.0).astype(jnp.bfloat16).reshape(token_count, KVW)
    )
    grad_value_lin = grad_values_rows.astype(jnp.bfloat16).reshape(token_count, KVW)
    grad_normed = (
        back_product(grad_query_lin, w_query)
        + back_product(grad_key_lin, w_key)
        + back_product(grad_value_lin, w_value)
    )
    norm_part_first, gain_first_grad = norm_backward(
        token_rows, inverse_first, gain_first, grad_normed
    )
    grad_tokens = (grad_middle + norm_part_first).reshape(seq_count, rows_local, D)
    small_partial = jnp.concatenate(
        [
            gain_first_grad,
            gain_second_grad,
            jnp.sum(grad_query_lin, axis=0, dtype=jnp.float32),
            jnp.sum(grad_key_lin, axis=0, dtype=jnp.float32),
            jnp.sum(grad_value_lin, axis=0, dtype=jnp.float32),
        ]
    )
    grad_small = exchange_sum(small_partial.reshape(all_count, -1), ALL_AXES)
    grad_lines = spread(
        jnp.concatenate([grad_query_lin, grad_key_lin, grad_value_lin], axis=1), "blk"
    ).reshape(blk_count * token_count, QW + 2 * KVW)
    middle_lines = spread(grad_middle_low, "blk").reshape(blk_count * token_count, D)
    attn_grads = jnp.concatenate(
        [
            matrix_to_tiles(
                outer_product(split_columns(normed, blk_count, shard_rows), grad_lines)
            ),
            matrix_to_tiles(
                outer_product(split_columns(out_rows, blk_count, shard_rows), middle_lines)
            ),
        ],
        axis=0,
    )
    attn_returned = attn_route.send_home(attn_route.home_buffer(attn_grads))
    my_slots = my_first + jnp.arange(slot_local, dtype=jnp.int32)
    slot_index = locate(my_slots, route.owner, route.slot_position()) + locate(
        my_slots, attn_route.owner, blk_count * route.pair_cap + attn_route.slot_position()
    )
    slot_used = jnp.any(my_slots[:, None] == owner_slot[None, :], axis=1)

    def routed_grads():
        return pick(jnp.concatenate([returned_grads, attn_returned], axis=0), slot_index)

    def summed_grads():
        every_slot = jnp.arange(slot_total, dtype=jnp.int32)
        tile_owner = jnp.concatenate([route.my_owner, attn_route.my_owner])
        index = locate(every_slot, tile_owner, jnp.arange(tile_owner.shape[0], dtype=jnp.int32))
        held = jnp.any(every_slot[:, None] == tile_owner[None, :], axis=1)
        parts = pick(jnp.concatenate([shard_grads, attn_grads], axis=0), index)
        parts = jnp.where(held[:, None, None], parts, 0)
        return lax.psum_scatter(parts, ALL_AXES, scatter_dimension=0, tiled=True)

    grad_slots = lax.cond(route.fits & attn_route.fits, routed_grads, summed_grads)
    grad_slots = jnp.where(slot_used[:, None, None], grad_slots, 0).astype(jnp.float32)
    rotated = jnp.einsum("sji,sjk->sik", basis_left, grad_slots, precision=TOP_PRECISION)
    rotated = jnp.einsum("sik,skl->sil", rotated, basis_right, precision=TOP_PRECISION)
    first_new = BETA_FIRST * moment_first + (1.0 - BETA_FIRST) * rotated
    second_new = BETA_SECOND * moment_second + (1.0 - BETA_SECOND) * rotated * rotated
    normalized = first_new / (jnp.sqrt(second_new) + ADAM_EPS)
    update = jnp.einsum("sik,skl->sil", basis_left, normalized, precision=TOP_PRECISION)
    update = jnp.einsum("sik,slk->sil", update, basis_right, precision=TOP_PRECISION)
    tile_scale = jnp.sqrt(jnp.mean(master * master, axis=(1, 2), keepdims=True) + SCALE_EPS)
    master_new = master - RELATIVE_RATE * tile_scale * (update + WEIGHT_DECAY * master)
    small_first_new = BETA_FIRST * small_first + (1.0 - BETA_FIRST) * grad_small
    small_second_new = BETA_SECOND * small_second + (1.0 - BETA_SECOND) * grad_small * grad_small
    small_new = small_master - SMALL_RATE * (
        small_first_new / (jnp.sqrt(small_second_new) + ADAM_EPS) + WEIGHT_DECAY * small_master
    )
    return (
        mixed_out,
        grad_tokens,
        first_new,
        second_new,
        master_new,
        small_first_new,
        small_second_new,
        small_new,
    )


def solution(mesh):
    in_specs = (
        P("dp", ("blk", "uly"), None),
        P("dp", ("blk", "uly"), None),
        P("dp"),
        P(),
        P(("dp", "blk", "uly"), None, None),
        P(("dp", "blk", "uly"), None, None),
        P(("dp", "blk", "uly"), None, None),
        P(("dp", "blk", "uly"), None, None),
        P(("dp", "blk", "uly"), None, None),
        P(("dp", "blk", "uly")),
        P(("dp", "blk", "uly")),
        P(("dp", "blk", "uly")),
    )
    out_specs = (
        P("dp", ("blk", "uly"), None),
        P("dp", ("blk", "uly"), None),
        P(("dp", "blk", "uly"), None, None),
        P(("dp", "blk", "uly"), None, None),
        P(("dp", "blk", "uly"), None, None),
        P(("dp", "blk", "uly")),
        P(("dp", "blk", "uly")),
        P(("dp", "blk", "uly")),
    )
    return jax.shard_map(local, mesh=mesh, in_specs=in_specs, out_specs=out_specs, check_vma=False)
```

```python
import math

import jax
import jax.numpy as jnp
import numpy as np
from jax import lax
from jax.experimental import pallas as pl
from jax.experimental.pallas import tpu as pltpu
from jax.sharding import PartitionSpec as P

D = 1536
QH = 12
KVH = 2
HD = 128
FF = 8960
BLOCK = 128
QW = 1536
KVW = 256


NORM_EPS = 1e-06
ROPE_BASE = 1000000.0
BETA_FIRST = 0.5
BETA_SECOND = 0.5
ADAM_EPS = 1e-08
SCALE_EPS = 1e-06
RELATIVE_RATE = 0.5
SMALL_RATE = 0.25
WEIGHT_DECAY = 0.01
MASK_FILL = -1e30


def matrix_shapes():
    return [(D, QW), (D, KVW), (D, KVW), (QW, D), (D, FF), (D, FF), (FF, D)]


def split_small(vector):
    edges = [0, D, 2 * D, 2 * D + QW, 2 * D + QW + KVW, 2 * D + QW + 2 * KVW]
    return [vector[edges[number] : edges[number + 1]] for number in range(5)]


GRID_D = D // BLOCK
GRID_FF = FF // BLOCK
ATTN_TILES = GRID_D * (QW + 2 * KVW) // BLOCK + QW // BLOCK * GRID_D
ALL_AXES = ("dp", "blk", "uly")
COLUMN_AXES = ("dp", "uly")


def capacity(mean, factor, limit):
    return int(min(limit, math.ceil(mean + factor * math.sqrt(mean))))


def pick(table, index):
    return jnp.take(table, index, axis=0, mode="clip")


def earlier_equal(keys):
    number = jnp.arange(keys.shape[0], dtype=jnp.int32)
    same = keys[None, :] == keys[:, None]
    return jnp.sum((same & (number[None, :] < number[:, None])).astype(jnp.int32), axis=1)


def locate(wanted, keys, values):
    return jnp.sum(jnp.where(wanted[:, None] == keys[None, :], values[None, :], 0), axis=1)


def tiles_to_matrix(tiles, row_tiles, col_tiles):
    blocked = tiles.reshape(row_tiles, col_tiles, BLOCK, BLOCK)
    return blocked.transpose(0, 2, 1, 3).reshape(row_tiles * BLOCK, col_tiles * BLOCK)


def matrix_to_tiles(matrix):
    row_tiles = matrix.shape[0] // BLOCK
    col_tiles = matrix.shape[1] // BLOCK
    blocked = matrix.reshape(row_tiles, BLOCK, col_tiles, BLOCK)
    return blocked.transpose(0, 2, 1, 3).reshape(row_tiles * col_tiles, BLOCK, BLOCK)


def exchange(values, axes):
    return lax.all_to_all(values, axes, split_axis=0, concat_axis=0, tiled=True)


def spread(values, axes):
    count = lax.axis_size(axes)
    return exchange(jnp.broadcast_to(values[None], (count,) + values.shape), axes)


def exchange_sum(values, axes):
    return jnp.sum(exchange(values, axes).astype(jnp.float32), axis=0)


STEP_GROUPS = 2
STEP_TILES = 3 * STEP_GROUPS * GRID_D
STEP_COLUMNS = STEP_GROUPS * BLOCK
ROW_CHUNK = 512


def shard_owners(owner_slot, shard_count, shard_groups):
    missing = shard_count * shard_groups - GRID_FF
    first = ATTN_TILES
    members = []
    for number in range(3):
        grid = owner_slot[first : first + GRID_D * GRID_FF]
        if number < 2:
            grid = grid.reshape(GRID_D, GRID_FF).transpose(1, 0)
        else:
            grid = grid.reshape(GRID_FF, GRID_D)
        grid = jnp.pad(grid, ((0, missing), (0, 0)), constant_values=-1)
        members.append(
            grid.reshape(shard_count, shard_groups // STEP_GROUPS, STEP_GROUPS * GRID_D)
        )
        first = first + GRID_D * GRID_FF
    return jnp.stack(members, axis=2).reshape(shard_count, -1)


def mix_kernel(first_ref, x_ref, xt_ref, seed_ref, w_ref, tiles_ref, grad_ref, mixed_ref, acc_grad, acc_mixed):
    step = pl.program_id(0)
    kind = STEP_GROUPS * GRID_D

    @pl.when(step == 0)
    def _():
        acc_grad[...] = jnp.zeros_like(acc_grad)
        acc_mixed[...] = jnp.zeros_like(acc_mixed)

    def tall(first):
        return jnp.concatenate(
            [
                w_ref[first + group * GRID_D : first + (group + 1) * GRID_D].reshape(D, BLOCK)
                for group in range(STEP_GROUPS)
            ],
            axis=1,
        )

    def product(left, right, dims):
        return lax.dot_general(left, right, (dims, ((), ())), preferred_element_type=jnp.float32)

    w_gate = tall(0)
    w_up = tall(kind)
    w_down = jnp.concatenate(
        [
            jnp.concatenate(
                [w_ref[2 * kind + group * GRID_D + col] for col in range(GRID_D)], axis=1
            )
            for group in range(STEP_GROUPS)
        ],
        axis=0,
    )
    rows = x_ref.shape[0]
    real_columns = (GRID_FF - first_ref[0] - step * STEP_GROUPS) * BLOCK
    real = lax.broadcasted_iota(jnp.int32, (rows, STEP_COLUMNS), 1) < real_columns
    x = x_ref[...]
    seed = seed_ref[...]
    gate = product(x, w_gate, ((1,), (0,)))
    upward = product(x, w_up, ((1,), (0,)))
    grad_hidden = product(seed, w_down, ((1,), (1,)))
    sig = 1.0 / (1.0 + jnp.exp(-gate))
    silu = gate * sig
    hidden = jnp.where(real, silu * upward, 0.0).astype(jnp.bfloat16)
    grad_gate = jnp.where(
        real, grad_hidden * upward * sig * (1.0 + gate * (1.0 - sig)), 0.0
    ).astype(jnp.bfloat16)
    grad_up = jnp.where(real, grad_hidden * silu, 0.0).astype(jnp.bfloat16)
    acc_grad[...] += product(grad_gate, w_gate, ((1,), (1,))) + product(
        grad_up, w_up, ((1,), (1,))
    )
    acc_mixed[...] += product(hidden, w_down, ((1,), (0,)))
    xt = xt_ref[...]
    for number, right in ((0, grad_gate), (1, grad_up)):
        part = product(xt, right, ((1,), (0,))).astype(jnp.bfloat16)
        for group in range(STEP_GROUPS):
            first = number * kind + group * GRID_D
            tiles_ref[first : first + GRID_D] = part[
                :, group * BLOCK : (group + 1) * BLOCK
            ].reshape(GRID_D, BLOCK, BLOCK)
    part = product(hidden, seed, ((0,), (0,))).astype(jnp.bfloat16)
    for group in range(STEP_GROUPS):
        for col in range(GRID_D):
            tiles_ref[2 * kind + group * GRID_D + col] = part[
                group * BLOCK : (group + 1) * BLOCK, col * BLOCK : (col + 1) * BLOCK
            ]

    @pl.when(step == pl.num_programs(0) - 1)
    def _():
        grad_ref[...] = acc_grad[...].astype(grad_ref.dtype)
        mixed_ref[...] = acc_mixed[...].astype(mixed_ref.dtype)


def mix_chunk(first_group, x, seed, stack):
    rows = x.shape[0]
    steps = stack.shape[0] // STEP_TILES

    def fixed(shape):
        return pl.BlockSpec(shape, lambda step, first: (0,) * len(shape))

    tiles = pl.BlockSpec((STEP_TILES, BLOCK, BLOCK), lambda step, first: (step, 0, 0))
    return pl.pallas_call(
        mix_kernel,
        out_shape=(
            jax.ShapeDtypeStruct(stack.shape, jnp.bfloat16),
            jax.ShapeDtypeStruct((rows, D), jnp.bfloat16),
            jax.ShapeDtypeStruct((rows, D), jnp.bfloat16),
        ),
        grid_spec=pltpu.PrefetchScalarGridSpec(
            num_scalar_prefetch=1,
            grid=(steps,),
            in_specs=[fixed((rows, D)), fixed((D, rows)), fixed((rows, D)), tiles],
            out_specs=(tiles, fixed((rows, D)), fixed((rows, D))),
            scratch_shapes=[pltpu.VMEM((rows, D), jnp.float32), pltpu.VMEM((rows, D), jnp.float32)],
        ),
        compiler_params=pltpu.CompilerParams(
            dimension_semantics=("arbitrary",), vmem_limit_bytes=56 * 1024 * 1024
        ),
    )(first_group, x, x.T, seed, stack)


def mix_lines(first_group, x, seed, stack):
    parts = []
    for first in range(0, x.shape[0], ROW_CHUNK):
        last = min(first + ROW_CHUNK, x.shape[0])
        parts.append(mix_chunk(first_group, x[first:last], seed[first:last], stack))
    if len(parts) == 1:
        return parts[0]
    tiles = sum(part[0].astype(jnp.float32) for part in parts).astype(jnp.bfloat16)
    return (
        tiles,
        jnp.concatenate([part[1] for part in parts], axis=0),
        jnp.concatenate([part[2] for part in parts], axis=0),
    )


def attention_owners(owner_slot, shard_count, shard_rows):
    grids = []
    first = 0
    for row_count, col_count in matrix_shapes()[:4]:
        tile_count = row_count // BLOCK * (col_count // BLOCK)
        grids.append(owner_slot[first : first + tile_count].reshape(row_count // BLOCK, -1))
        first = first + tile_count
    members = []
    for grid in (jnp.concatenate(grids[:3], axis=1), grids[3]):
        missing = shard_count * shard_rows - grid.shape[0]
        grid = jnp.pad(grid, ((0, missing), (0, 0)), constant_values=-1)
        members.append(grid.reshape(shard_count, -1))
    return jnp.concatenate(members, axis=1)


def split_columns(values, shard_count, shard_rows):
    width = shard_rows * BLOCK
    padded = jnp.pad(values, ((0, 0), (0, shard_count * width - values.shape[1])))
    parts = padded.reshape(values.shape[0], shard_count, width).transpose(1, 0, 2)
    return exchange(parts, "blk").reshape(-1, width)


class Route:
    def __init__(self, owners, slot_local, factors):
        uly_count = lax.axis_size("uly")
        blk_count = lax.axis_size("blk")
        blk_index = lax.axis_index("blk")
        self.column_count = lax.axis_size("dp") * uly_count
        self.column = lax.axis_index("dp") * uly_count + lax.axis_index("uly")
        self.device = (lax.axis_index("dp") * blk_count + blk_index) * uly_count + lax.axis_index(
            "uly"
        )
        self.tiles = owners.shape[1]
        self.pair_cap = capacity(self.tiles / (self.column_count * blk_count), factors[0], slot_local)
        self.column_cap = capacity(self.tiles / self.column_count, factors[1], self.tiles)
        flat = owners.reshape(-1)
        self.owner = flat
        self.first = self.device * slot_local
        self.real = flat >= 0
        self.shard = jnp.repeat(jnp.arange(blk_count, dtype=jnp.int32), self.tiles)
        self.holder = jnp.maximum(flat, 0) // slot_local
        columns = self.holder // (blk_count * uly_count) * uly_count + self.holder % uly_count
        source = self.holder // uly_count % blk_count
        self.pair_rank = earlier_equal(jnp.where(self.real, self.holder * blk_count + self.shard, -1))
        line_rank = earlier_equal(jnp.where(self.real, columns * blk_count + self.shard, -1))
        self.fits = (jnp.max(jnp.where(self.real, self.pair_rank, 0)) < self.pair_cap) & (
            jnp.max(jnp.where(self.real, line_rank, 0)) < self.column_cap
        )

        def mine(values):
            return lax.dynamic_slice_in_dim(values, blk_index * self.tiles, self.tiles, 0)

        self.my_owner = mine(flat)
        self.my_rank = mine(line_rank)
        my_real = mine(self.real)
        my_columns = mine(columns)
        my_pair_rank = mine(self.pair_rank)
        self.place = jnp.where(my_real, my_columns * self.column_cap + self.my_rank, -1)
        self.held = my_real & (my_columns == self.column) & (my_pair_rank < self.pair_cap)
        self.arrival = mine(source) * self.pair_cap + my_pair_rank
        self.pair_slots = jnp.arange(blk_count * self.pair_cap, dtype=jnp.int32)

    def slot_position(self):
        return self.shard * self.pair_cap + self.pair_rank

    def send_index(self):
        key = jnp.where(
            self.real & (self.holder == self.device) & (self.pair_rank < self.pair_cap),
            self.slot_position(),
            -1,
        )
        return locate(self.pair_slots, key, self.owner - self.first)

    def compact_index(self):
        wanted = jnp.arange(self.column_cap, dtype=jnp.int32)
        return locate(wanted, jnp.where(self.held, self.my_rank, -1), self.arrival)

    def home_buffer(self, tiles):
        wanted = jnp.arange(self.column_count * self.column_cap, dtype=jnp.int32)
        index = locate(wanted, self.place, jnp.arange(self.tiles, dtype=jnp.int32))
        return pick(tiles, index)

    def sum_columns(self, buffer):
        return lax.psum_scatter(buffer, COLUMN_AXES, scatter_dimension=0, tiled=True)

    def send_home(self, summed):
        back = locate(self.pair_slots, jnp.where(self.held, self.arrival, -1), self.my_rank)
        return exchange(pick(summed, back), "blk")


def soap_kernel(
    used_ref, grad_ref, master_ref, first_ref, second_ref, left_ref, right_ref,
    master_out, first_out, second_out,
):
    count = grad_ref.shape[0]
    base = pl.program_id(0) * count

    def product(one, other, dims):
        return lax.dot_general(
            one.astype(jnp.bfloat16),
            other.astype(jnp.bfloat16),
            (dims, ((), ())),
            preferred_element_type=jnp.float32,
        )

    for number in range(count):
        grad = jnp.where(used_ref[base + number] > 0, grad_ref[number], jnp.bfloat16(0))
        left = left_ref[number].astype(jnp.bfloat16)
        right = right_ref[number].astype(jnp.bfloat16)
        rotated = product(product(left, grad, ((0,), (0,))), right, ((1,), (0,)))
        first_new = BETA_FIRST * first_ref[number] + (1.0 - BETA_FIRST) * rotated
        second_new = BETA_SECOND * second_ref[number] + (1.0 - BETA_SECOND) * rotated * rotated
        normalized = first_new / (jnp.sqrt(second_new) + ADAM_EPS)
        update = product(product(left, normalized, ((1,), (0,))), right, ((1,), (1,)))
        master = master_ref[number]
        scale = jnp.sqrt(jnp.mean(master * master, keepdims=True) + SCALE_EPS)
        first_out[number] = first_new
        second_out[number] = second_new
        master_out[number] = master - RELATIVE_RATE * scale * (update + WEIGHT_DECAY * master)


def soap_step(used, grads, *state):
    slots = grads.shape[0]
    count = max(number for number in range(1, 11) if slots % number == 0)
    tiles = pl.BlockSpec((count, BLOCK, BLOCK), lambda step, flags: (step, 0, 0))
    whole = jax.ShapeDtypeStruct((slots, BLOCK, BLOCK), jnp.float32)
    return pl.pallas_call(
        soap_kernel,
        out_shape=(whole, whole, whole),
        grid_spec=pltpu.PrefetchScalarGridSpec(
            num_scalar_prefetch=1,
            grid=(slots // count,),
            in_specs=[tiles] * 6,
            out_specs=(tiles, tiles, tiles),
        ),
        compiler_params=pltpu.CompilerParams(
            dimension_semantics=("arbitrary",), vmem_limit_bytes=40 * 1024 * 1024
        ),
    )(used, grads, *state)


def rotate(values, positions, direction):
    half_size = HD // 2
    frequency = ROPE_BASE ** (-2.0 * jnp.arange(half_size, dtype=jnp.float32) / HD)
    angles = positions.astype(jnp.float32)[:, None] * frequency[None, :]
    cosine = jnp.cos(angles)[:, None, :]
    sine = direction * jnp.sin(angles)[:, None, :]
    first_half = values[..., :half_size]
    second_half = values[..., half_size:]
    return jnp.concatenate(
        [first_half * cosine - second_half * sine, second_half * cosine + first_half * sine],
        axis=-1,
    )


def forward_product(left_side, weight):
    return jnp.dot(left_side, weight, preferred_element_type=jnp.float32)


def back_product(grads, weight):
    return jnp.einsum("nf,df->nd", grads, weight, preferred_element_type=jnp.float32)


def outer_product(left_side, right_side):
    return jnp.einsum(
        "nb,nc->bc", left_side, right_side, preferred_element_type=jnp.float32
    ).astype(jnp.bfloat16)


def norm_backward(values, inverse, gain, grad_normed):
    scaled = values * inverse
    gained = grad_normed * gain
    grad_values = inverse * (gained - scaled * jnp.mean(gained * scaled, axis=-1, keepdims=True))
    return (grad_values, jnp.sum(grad_normed * scaled, axis=0))


def local(
    tokens,
    cotangent,
    lengths,
    owner_slot,
    master,
    moment_first,
    moment_second,
    basis_left,
    basis_right,
    small_master,
    small_first,
    small_second,
):
    uly_count = lax.axis_size("uly")
    blk_count = lax.axis_size("blk")
    all_count = lax.axis_size("dp") * blk_count * uly_count
    uly_index = lax.axis_index("uly")
    blk_index = lax.axis_index("blk")
    seq_count = tokens.shape[0]
    rows_local = tokens.shape[1]
    token_count = seq_count * rows_local
    span_rows = rows_local * uly_count
    heads_local = QH // uly_count
    slot_local = master.shape[0]
    slot_total = slot_local * all_count
    score_root = math.sqrt(HD)
    positions = (blk_index * uly_count + uly_index) * rows_local + jnp.arange(
        rows_local, dtype=jnp.int32
    )
    query_pos = blk_index * span_rows + jnp.arange(span_rows, dtype=jnp.int32)
    head_of = [member * heads_local // (QH // KVH) for member in range(uly_count)]
    shard_groups = -(-GRID_FF // (blk_count * STEP_GROUPS)) * STEP_GROUPS
    shard_rows = -(-GRID_D // blk_count)
    attn_cap = capacity(ATTN_TILES / all_count, 3.8, slot_local)
    route = Route(shard_owners(owner_slot, blk_count, shard_groups), slot_local, (3.5, 3.45))
    attn_route = Route(attention_owners(owner_slot, blk_count, shard_rows), slot_local, (5.0, 3.8))
    my_first = route.first
    attn_owner = owner_slot[:ATTN_TILES]
    attn_device = attn_owner // slot_local
    attn_rank = earlier_equal(attn_device)
    fits_attn = jnp.max(attn_rank) < attn_cap
    attn_send = locate(
        jnp.arange(attn_cap, dtype=jnp.int32),
        jnp.where(attn_device == route.device, attn_rank, -1),
        attn_owner - my_first,
    )
    attn_place = attn_device * attn_cap + attn_rank

    master_low = master.astype(jnp.bfloat16)
    small_copies = spread(small_master.astype(jnp.bfloat16), ALL_AXES).reshape(-1)
    attn_gathered = lax.all_gather(pick(master_low, attn_send), ALL_AXES, axis=0, tiled=True)

    def whole_tiles(index):
        return pick(lax.all_gather(master_low, ALL_AXES, axis=0, tiled=True), index)

    attn_tiles = lax.cond(
        fits_attn, lambda: pick(attn_gathered, attn_place), lambda: whole_tiles(attn_owner)
    )
    arrived_tiles = exchange(pick(master_low, route.send_index()), "blk")
    shard_buffer = lax.all_gather(
        pick(arrived_tiles, route.compact_index()), COLUMN_AXES, axis=0, tiled=True
    )
    shard_stack = lax.cond(
        route.fits, lambda: pick(shard_buffer, route.place), lambda: whole_tiles(route.my_owner)
    )
    attn_matrices = []
    first = 0
    for row_count, col_count in matrix_shapes()[:4]:
        tile_count = row_count // BLOCK * (col_count // BLOCK)
        attn_matrices.append(
            tiles_to_matrix(
                attn_tiles[first : first + tile_count], row_count // BLOCK, col_count // BLOCK
            )
        )
        first = first + tile_count
    w_query, w_key, w_value, w_out = attn_matrices
    smalls = [member.astype(jnp.float32) for member in split_small(small_copies)]
    gain_first, gain_second, bias_query, bias_key, bias_value = smalls
    valid_rows = (positions[None, :] < lengths[:, None]).astype(jnp.float32)
    seed_grad = (cotangent.astype(jnp.float32) * valid_rows[:, :, None]).reshape(token_count, D)
    seed_low = seed_grad.astype(jnp.bfloat16)
    seed_line = spread(seed_low, "blk").reshape(blk_count * token_count, D)
    token_rows = tokens.reshape(token_count, D).astype(jnp.float32)
    inverse_first = lax.rsqrt(jnp.mean(token_rows * token_rows, axis=-1, keepdims=True) + NORM_EPS)
    normed = (token_rows * inverse_first * gain_first).astype(jnp.bfloat16)
    query_lin = forward_product(normed, w_query) + bias_query
    key_lin = forward_product(normed, w_key) + bias_key
    value_rows = (
        (forward_product(normed, w_value) + bias_value)
        .astype(jnp.bfloat16)
        .reshape(seq_count, rows_local, KVH, HD)
    )
    query_rot = rotate(query_lin.reshape(seq_count, rows_local, QH, HD), positions, 1.0).astype(
        jnp.bfloat16
    )
    key_rot = rotate(key_lin.reshape(seq_count, rows_local, KVH, HD), positions, 1.0).astype(
        jnp.bfloat16
    )
    query_heads = lax.all_to_all(query_rot, "uly", split_axis=2, concat_axis=1, tiled=True)
    key_value = jnp.concatenate([key_rot, value_rows], axis=-1)
    key_value = jnp.stack([key_value[:, :, head] for head in head_of], axis=0)
    key_value = exchange(key_value, "uly").transpose(1, 0, 2, 3)
    key_value = spread(key_value, "blk").transpose(1, 0, 2, 3, 4)
    key_value = key_value.reshape(seq_count, blk_count * span_rows, 2 * HD)
    keys = key_value[..., :HD]
    values = key_value[..., HD:]
    key_pos = jnp.arange(blk_count * span_rows, dtype=jnp.int32)
    allowed = (key_pos[None, None, :] <= query_pos[None, :, None]) & (
        key_pos[None, None, :] < lengths[:, None, None]
    )
    allowed = allowed[:, :, None, :]
    scores = (
        jnp.einsum("sqhd,skd->sqhk", query_heads, keys, preferred_element_type=jnp.float32)
        / score_root
    )
    scores = jnp.where(allowed, scores, MASK_FILL)
    top = jnp.max(scores, axis=-1, keepdims=True)
    weights = jnp.where(allowed, jnp.exp(scores - top), 0.0)
    probs = weights / jnp.sum(weights, axis=-1, keepdims=True)
    probs_low = probs.astype(jnp.bfloat16)
    attended = jnp.einsum(
        "sqhk,skd->sqhd", probs_low, values, preferred_element_type=jnp.float32
    )
    out_rows = lax.all_to_all(
        attended.astype(jnp.bfloat16), "uly", split_axis=1, concat_axis=2, tiled=True
    ).reshape(token_count, QW)
    middle = token_rows + forward_product(out_rows, w_out)
    inverse_second = lax.rsqrt(jnp.mean(middle * middle, axis=-1, keepdims=True) + NORM_EPS)
    normed_two = (middle * inverse_second * gain_second).astype(jnp.bfloat16)
    normed_line = spread(normed_two, "blk").reshape(blk_count * token_count, D)
    first_group = jnp.full((1,), blk_index * shard_groups, jnp.int32)
    shard_grads, grad_line, mixed_line = mix_lines(
        first_group, normed_line, seed_line, shard_stack
    )
    grad_normed_two = exchange_sum(grad_line.reshape(blk_count, token_count, D), "blk")
    home_buffer = route.home_buffer(shard_grads)
    grad_normed_two, home_buffer = lax.optimization_barrier((grad_normed_two, home_buffer))
    summed_tiles = route.sum_columns(home_buffer)
    norm_part_two, gain_second_grad = norm_backward(
        middle, inverse_second, gain_second, grad_normed_two
    )
    grad_middle = seed_grad + norm_part_two
    grad_middle_low = grad_middle.astype(jnp.bfloat16)
    grad_out_rows = (
        back_product(grad_middle_low, w_out)
        .astype(jnp.bfloat16)
        .reshape(seq_count, rows_local, QH, HD)
    )
    grad_heads = lax.all_to_all(grad_out_rows, "uly", split_axis=2, concat_axis=1, tiled=True)
    grad_heads_wide = grad_heads.astype(jnp.float32)
    row_delta = jnp.sum(grad_heads_wide * attended, axis=-1)

    grad_prob = jnp.einsum(
        "sqhd,skd->sqhk", grad_heads, values, preferred_element_type=jnp.float32
    )
    grad_score = (probs * (grad_prob - row_delta[..., None])).astype(jnp.bfloat16)
    grad_query = jnp.einsum(
        "sqhk,skd->sqhd", grad_score, keys, preferred_element_type=jnp.float32
    )
    grad_keys = jnp.einsum(
        "sqhk,sqhd->skd", grad_score, query_heads, preferred_element_type=jnp.float32
    )
    grad_values = jnp.einsum(
        "sqhk,sqhd->skd", probs_low, grad_heads, preferred_element_type=jnp.float32
    )
    grad_query_low = (grad_query / score_root).astype(jnp.bfloat16)
    grad_query_rows = lax.all_to_all(grad_query_low, "uly", split_axis=1, concat_axis=2, tiled=True)
    grad_pair = jnp.concatenate([grad_keys / score_root, grad_values], axis=-1).astype(jnp.bfloat16)
    grad_pair = grad_pair.reshape(seq_count, blk_count, span_rows, 2 * HD).transpose(1, 0, 2, 3)
    grad_pair = exchange_sum(grad_pair, "blk").astype(jnp.bfloat16)
    grad_pair = grad_pair.reshape(seq_count, uly_count, rows_local, 2 * HD).transpose(1, 0, 2, 3)
    grad_pair = exchange(grad_pair, "uly").astype(jnp.float32)
    grad_pair = jnp.stack(
        [
            sum(grad_pair[member] for member in range(uly_count) if head_of[member] == head)
            for head in range(KVH)
        ],
        axis=2,
    )
    grad_keys_rows = grad_pair[..., :HD]
    grad_values_rows = grad_pair[..., HD:]
    grad_query_lin = (
        rotate(grad_query_rows.astype(jnp.float32), positions, -1.0)
        .astype(jnp.bfloat16)
        .reshape(token_count, QW)
    )
    key_rounded = grad_keys_rows
    grad_key_lin = (
        rotate(key_rounded, positions, -1.0).astype(jnp.bfloat16).reshape(token_count, KVW)
    )
    grad_value_lin = grad_values_rows.astype(jnp.bfloat16).reshape(token_count, KVW)
    grad_normed = (
        back_product(grad_query_lin, w_query)
        + back_product(grad_key_lin, w_key)
        + back_product(grad_value_lin, w_value)
    )
    norm_part_first, gain_first_grad = norm_backward(
        token_rows, inverse_first, gain_first, grad_normed
    )
    grad_tokens = (grad_middle + norm_part_first).reshape(seq_count, rows_local, D)
    small_partial = jnp.concatenate(
        [
            gain_first_grad,
            gain_second_grad,
            jnp.sum(grad_query_lin, axis=0, dtype=jnp.float32),
            jnp.sum(grad_key_lin, axis=0, dtype=jnp.float32),
            jnp.sum(grad_value_lin, axis=0, dtype=jnp.float32),
        ]
    )
    grad_small = exchange_sum(small_partial.reshape(all_count, -1), ALL_AXES)
    grad_lines = spread(
        jnp.concatenate([grad_query_lin, grad_key_lin, grad_value_lin], axis=1), "blk"
    ).reshape(blk_count * token_count, QW + 2 * KVW)
    returned_grads = route.send_home(summed_tiles)
    grad_lines, mixed_line = lax.optimization_barrier((grad_lines, mixed_line))
    mixed_out = (
        (middle + exchange_sum(mixed_line.reshape(blk_count, token_count, D), "blk"))
        .astype(jnp.bfloat16)
        .reshape(seq_count, rows_local, D)
    )
    middle_lines = spread(grad_middle_low, "blk").reshape(blk_count * token_count, D)
    attn_grads = jnp.concatenate(
        [
            matrix_to_tiles(
                outer_product(split_columns(normed, blk_count, shard_rows), grad_lines)
            ),
            matrix_to_tiles(
                outer_product(split_columns(out_rows, blk_count, shard_rows), middle_lines)
            ),
        ],
        axis=0,
    )
    attn_buffer = attn_route.home_buffer(attn_grads)
    attn_buffer, summed_tiles = lax.optimization_barrier((attn_buffer, summed_tiles))
    attn_returned = attn_route.send_home(attn_route.sum_columns(attn_buffer))
    my_slots = my_first + jnp.arange(slot_local, dtype=jnp.int32)
    slot_index = locate(my_slots, route.owner, route.slot_position()) + locate(
        my_slots, attn_route.owner, blk_count * route.pair_cap + attn_route.slot_position()
    )
    slot_used = jnp.any(my_slots[:, None] == owner_slot[None, :], axis=1)

    def routed_grads():
        return pick(jnp.concatenate([returned_grads, attn_returned], axis=0), slot_index)

    def summed_grads():
        every_slot = jnp.arange(slot_total, dtype=jnp.int32)
        tile_owner = jnp.concatenate([route.my_owner, attn_route.my_owner])
        index = locate(every_slot, tile_owner, jnp.arange(tile_owner.shape[0], dtype=jnp.int32))
        held = jnp.any(every_slot[:, None] == tile_owner[None, :], axis=1)
        parts = pick(jnp.concatenate([shard_grads, attn_grads], axis=0), index)
        parts = jnp.where(held[:, None, None], parts, 0)
        return lax.psum_scatter(parts, ALL_AXES, scatter_dimension=0, tiled=True)

    grad_slots = lax.cond(route.fits & attn_route.fits, routed_grads, summed_grads)
    master_new, first_new, second_new = soap_step(
        slot_used.astype(jnp.int32),
        grad_slots,
        master,
        moment_first,
        moment_second,
        basis_left,
        basis_right,
    )
    small_first_new = BETA_FIRST * small_first + (1.0 - BETA_FIRST) * grad_small
    small_second_new = BETA_SECOND * small_second + (1.0 - BETA_SECOND) * grad_small * grad_small
    small_new = small_master - SMALL_RATE * (
        small_first_new / (jnp.sqrt(small_second_new) + ADAM_EPS) + WEIGHT_DECAY * small_master
    )
    return (
        mixed_out,
        grad_tokens,
        first_new,
        second_new,
        master_new,
        small_first_new,
        small_second_new,
        small_new,
    )


def solution(mesh):
    in_specs = (
        P("dp", ("blk", "uly"), None),
        P("dp", ("blk", "uly"), None),
        P("dp"),
        P(),
        P(("dp", "blk", "uly"), None, None),
        P(("dp", "blk", "uly"), None, None),
        P(("dp", "blk", "uly"), None, None),
        P(("dp", "blk", "uly"), None, None),
        P(("dp", "blk", "uly"), None, None),
        P(("dp", "blk", "uly")),
        P(("dp", "blk", "uly")),
        P(("dp", "blk", "uly")),
    )
    out_specs = (
        P("dp", ("blk", "uly"), None),
        P("dp", ("blk", "uly"), None),
        P(("dp", "blk", "uly"), None, None),
        P(("dp", "blk", "uly"), None, None),
        P(("dp", "blk", "uly"), None, None),
        P(("dp", "blk", "uly")),
        P(("dp", "blk", "uly")),
        P(("dp", "blk", "uly")),
    )
    return jax.shard_map(local, mesh=mesh, in_specs=in_specs, out_specs=out_specs, check_vma=False)
```

```python
import math

import jax
import jax.numpy as jnp
import numpy as np
from jax import lax
from jax.experimental import pallas as pl
from jax.experimental.pallas import tpu as pltpu
from jax.sharding import PartitionSpec as P

D = 1536
QH = 12
KVH = 2
HD = 128
FF = 8960
BLOCK = 128
QW = 1536
KVW = 256


NORM_EPS = 1e-06
ROPE_BASE = 1000000.0
BETA_FIRST = 0.5
BETA_SECOND = 0.5
ADAM_EPS = 1e-08
SCALE_EPS = 1e-06
RELATIVE_RATE = 0.5
SMALL_RATE = 0.25
WEIGHT_DECAY = 0.01
MASK_FILL = -1e30


def matrix_shapes():
    return [(D, QW), (D, KVW), (D, KVW), (QW, D), (D, FF), (D, FF), (FF, D)]


def split_small(vector):
    edges = [0, D, 2 * D, 2 * D + QW, 2 * D + QW + KVW, 2 * D + QW + 2 * KVW]
    return [vector[edges[number] : edges[number + 1]] for number in range(5)]


GRID_D = D // BLOCK
GRID_FF = FF // BLOCK
ATTN_TILES = GRID_D * (QW + 2 * KVW) // BLOCK + QW // BLOCK * GRID_D
ALL_AXES = ("dp", "blk", "uly")
COLUMN_AXES = ("dp", "uly")


def capacity(mean, factor, limit):
    return int(min(limit, math.ceil(mean + factor * math.sqrt(mean))))


def pick(table, index):
    return jnp.take(table, index, axis=0, mode="clip")


def earlier_equal(keys):
    number = jnp.arange(keys.shape[0], dtype=jnp.int32)
    same = keys[None, :] == keys[:, None]
    return jnp.sum((same & (number[None, :] < number[:, None])).astype(jnp.int32), axis=1)


def locate(wanted, keys, values):
    return jnp.sum(jnp.where(wanted[:, None] == keys[None, :], values[None, :], 0), axis=1)


def tiles_to_matrix(tiles, row_tiles, col_tiles):
    blocked = tiles.reshape(row_tiles, col_tiles, BLOCK, BLOCK)
    return blocked.transpose(0, 2, 1, 3).reshape(row_tiles * BLOCK, col_tiles * BLOCK)


def matrix_to_tiles(matrix):
    row_tiles = matrix.shape[0] // BLOCK
    col_tiles = matrix.shape[1] // BLOCK
    blocked = matrix.reshape(row_tiles, BLOCK, col_tiles, BLOCK)
    return blocked.transpose(0, 2, 1, 3).reshape(row_tiles * col_tiles, BLOCK, BLOCK)


def exchange(values, axes):
    return lax.all_to_all(values, axes, split_axis=0, concat_axis=0, tiled=True)


def spread(values, axes):
    count = lax.axis_size(axes)
    return exchange(jnp.broadcast_to(values[None], (count,) + values.shape), axes)


def exchange_sum(values, axes):
    return jnp.sum(exchange(values, axes).astype(jnp.float32), axis=0)


STEP_GROUPS = 2
STEP_TILES = 3 * STEP_GROUPS * GRID_D
STEP_COLUMNS = STEP_GROUPS * BLOCK
ROW_CHUNK = 512


def shard_owners(owner_slot, shard_count, shard_groups):
    missing = shard_count * shard_groups - GRID_FF
    first = ATTN_TILES
    members = []
    for number in range(3):
        grid = owner_slot[first : first + GRID_D * GRID_FF]
        if number < 2:
            grid = grid.reshape(GRID_D, GRID_FF).transpose(1, 0)
        else:
            grid = grid.reshape(GRID_FF, GRID_D)
        grid = jnp.pad(grid, ((0, missing), (0, 0)), constant_values=-1)
        members.append(
            grid.reshape(shard_count, shard_groups // STEP_GROUPS, STEP_GROUPS * GRID_D)
        )
        first = first + GRID_D * GRID_FF
    return jnp.stack(members, axis=2).reshape(shard_count, -1)


def mix_kernel(first_ref, x_ref, xt_ref, seed_ref, w_ref, tiles_ref, grad_ref, mixed_ref, acc_grad, acc_mixed):
    step = pl.program_id(0)
    kind = STEP_GROUPS * GRID_D

    @pl.when(step == 0)
    def _():
        acc_grad[...] = jnp.zeros_like(acc_grad)
        acc_mixed[...] = jnp.zeros_like(acc_mixed)

    def tall(first):
        return jnp.concatenate(
            [
                w_ref[first + group * GRID_D : first + (group + 1) * GRID_D].reshape(D, BLOCK)
                for group in range(STEP_GROUPS)
            ],
            axis=1,
        )

    def product(left, right, dims):
        return lax.dot_general(left, right, (dims, ((), ())), preferred_element_type=jnp.float32)

    w_gate = tall(0)
    w_up = tall(kind)
    w_down = jnp.concatenate(
        [
            jnp.concatenate(
                [w_ref[2 * kind + group * GRID_D + col] for col in range(GRID_D)], axis=1
            )
            for group in range(STEP_GROUPS)
        ],
        axis=0,
    )
    rows = x_ref.shape[0]
    real_columns = (GRID_FF - first_ref[0] - step * STEP_GROUPS) * BLOCK
    real = lax.broadcasted_iota(jnp.int32, (rows, STEP_COLUMNS), 1) < real_columns
    x = x_ref[...]
    seed = seed_ref[...]
    gate = product(x, w_gate, ((1,), (0,)))
    upward = product(x, w_up, ((1,), (0,)))
    grad_hidden = product(seed, w_down, ((1,), (1,)))
    sig = 1.0 / (1.0 + jnp.exp(-gate))
    silu = gate * sig
    hidden = jnp.where(real, silu * upward, 0.0).astype(jnp.bfloat16)
    grad_gate = jnp.where(
        real, grad_hidden * upward * sig * (1.0 + gate * (1.0 - sig)), 0.0
    ).astype(jnp.bfloat16)
    grad_up = jnp.where(real, grad_hidden * silu, 0.0).astype(jnp.bfloat16)
    acc_grad[...] += product(grad_gate, w_gate, ((1,), (1,))) + product(
        grad_up, w_up, ((1,), (1,))
    )
    acc_mixed[...] += product(hidden, w_down, ((1,), (0,)))
    xt = xt_ref[...]
    for number, right in ((0, grad_gate), (1, grad_up)):
        part = product(xt, right, ((1,), (0,))).astype(jnp.bfloat16)
        for group in range(STEP_GROUPS):
            first = number * kind + group * GRID_D
            tiles_ref[first : first + GRID_D] = part[
                :, group * BLOCK : (group + 1) * BLOCK
            ].reshape(GRID_D, BLOCK, BLOCK)
    part = product(hidden, seed, ((0,), (0,))).astype(jnp.bfloat16)
    for group in range(STEP_GROUPS):
        for col in range(GRID_D):
            tiles_ref[2 * kind + group * GRID_D + col] = part[
                group * BLOCK : (group + 1) * BLOCK, col * BLOCK : (col + 1) * BLOCK
            ]

    @pl.when(step == pl.num_programs(0) - 1)
    def _():
        grad_ref[...] = acc_grad[...].astype(grad_ref.dtype)
        mixed_ref[...] = acc_mixed[...].astype(mixed_ref.dtype)


def mix_chunk(first_group, x, seed, stack):
    rows = x.shape[0]
    steps = stack.shape[0] // STEP_TILES

    def fixed(shape):
        return pl.BlockSpec(shape, lambda step, first: (0,) * len(shape))

    tiles = pl.BlockSpec((STEP_TILES, BLOCK, BLOCK), lambda step, first: (step, 0, 0))
    return pl.pallas_call(
        mix_kernel,
        out_shape=(
            jax.ShapeDtypeStruct(stack.shape, jnp.bfloat16),
            jax.ShapeDtypeStruct((rows, D), jnp.bfloat16),
            jax.ShapeDtypeStruct((rows, D), jnp.bfloat16),
        ),
        grid_spec=pltpu.PrefetchScalarGridSpec(
            num_scalar_prefetch=1,
            grid=(steps,),
            in_specs=[fixed((rows, D)), fixed((D, rows)), fixed((rows, D)), tiles],
            out_specs=(tiles, fixed((rows, D)), fixed((rows, D))),
            scratch_shapes=[pltpu.VMEM((rows, D), jnp.float32), pltpu.VMEM((rows, D), jnp.float32)],
        ),
        compiler_params=pltpu.CompilerParams(
            dimension_semantics=("arbitrary",), vmem_limit_bytes=56 * 1024 * 1024
        ),
    )(first_group, x, x.T, seed, stack)


def mix_lines(first_group, x, seed, stack):
    parts = []
    for first in range(0, x.shape[0], ROW_CHUNK):
        last = min(first + ROW_CHUNK, x.shape[0])
        parts.append(mix_chunk(first_group, x[first:last], seed[first:last], stack))
    if len(parts) == 1:
        return parts[0]
    tiles = sum(part[0].astype(jnp.float32) for part in parts).astype(jnp.bfloat16)
    return (
        tiles,
        jnp.concatenate([part[1] for part in parts], axis=0),
        jnp.concatenate([part[2] for part in parts], axis=0),
    )


def attention_owners(owner_slot, shard_count, shard_rows):
    grids = []
    first = 0
    for row_count, col_count in matrix_shapes()[:4]:
        tile_count = row_count // BLOCK * (col_count // BLOCK)
        grids.append(owner_slot[first : first + tile_count].reshape(row_count // BLOCK, -1))
        first = first + tile_count
    members = []
    for grid in (jnp.concatenate(grids[:3], axis=1), grids[3]):
        missing = shard_count * shard_rows - grid.shape[0]
        grid = jnp.pad(grid, ((0, missing), (0, 0)), constant_values=-1)
        members.append(grid.reshape(shard_count, -1))
    return jnp.concatenate(members, axis=1)


def split_columns(values, shard_count, shard_rows):
    width = shard_rows * BLOCK
    padded = jnp.pad(values, ((0, 0), (0, shard_count * width - values.shape[1])))
    parts = padded.reshape(values.shape[0], shard_count, width).transpose(1, 0, 2)
    return exchange(parts, "blk").reshape(-1, width)


class Route:
    def __init__(self, owners, slot_local, factors):
        uly_count = lax.axis_size("uly")
        blk_count = lax.axis_size("blk")
        blk_index = lax.axis_index("blk")
        self.column_count = lax.axis_size("dp") * uly_count
        self.column = lax.axis_index("dp") * uly_count + lax.axis_index("uly")
        self.device = (lax.axis_index("dp") * blk_count + blk_index) * uly_count + lax.axis_index(
            "uly"
        )
        self.tiles = owners.shape[1]
        self.pair_cap = capacity(self.tiles / (self.column_count * blk_count), factors[0], slot_local)
        self.column_cap = capacity(self.tiles / self.column_count, factors[1], self.tiles)
        flat = owners.reshape(-1)
        self.owner = flat
        self.first = self.device * slot_local
        self.real = flat >= 0
        self.shard = jnp.repeat(jnp.arange(blk_count, dtype=jnp.int32), self.tiles)
        self.holder = jnp.maximum(flat, 0) // slot_local
        columns = self.holder // (blk_count * uly_count) * uly_count + self.holder % uly_count
        source = self.holder // uly_count % blk_count
        self.pair_rank = earlier_equal(jnp.where(self.real, self.holder * blk_count + self.shard, -1))
        line_rank = earlier_equal(jnp.where(self.real, columns * blk_count + self.shard, -1))
        self.fits = (jnp.max(jnp.where(self.real, self.pair_rank, 0)) < self.pair_cap) & (
            jnp.max(jnp.where(self.real, line_rank, 0)) < self.column_cap
        )

        def mine(values):
            return lax.dynamic_slice_in_dim(values, blk_index * self.tiles, self.tiles, 0)

        self.my_owner = mine(flat)
        self.my_rank = mine(line_rank)
        my_real = mine(self.real)
        my_columns = mine(columns)
        my_pair_rank = mine(self.pair_rank)
        self.place = jnp.where(my_real, my_columns * self.column_cap + self.my_rank, -1)
        self.held = my_real & (my_columns == self.column) & (my_pair_rank < self.pair_cap)
        self.arrival = mine(source) * self.pair_cap + my_pair_rank
        self.pair_slots = jnp.arange(blk_count * self.pair_cap, dtype=jnp.int32)

    def slot_position(self):
        return self.shard * self.pair_cap + self.pair_rank

    def send_index(self):
        key = jnp.where(
            self.real & (self.holder == self.device) & (self.pair_rank < self.pair_cap),
            self.slot_position(),
            -1,
        )
        return locate(self.pair_slots, key, self.owner - self.first)

    def compact_index(self):
        wanted = jnp.arange(self.column_cap, dtype=jnp.int32)
        return locate(wanted, jnp.where(self.held, self.my_rank, -1), self.arrival)

    def home_buffer(self, tiles):
        wanted = jnp.arange(self.column_count * self.column_cap, dtype=jnp.int32)
        index = locate(wanted, self.place, jnp.arange(self.tiles, dtype=jnp.int32))
        return pick(tiles, index)

    def sum_columns(self, buffer):
        return lax.psum_scatter(buffer, COLUMN_AXES, scatter_dimension=0, tiled=True)

    def back_buffer(self, summed):
        back = locate(self.pair_slots, jnp.where(self.held, self.arrival, -1), self.my_rank)
        return pick(summed, back)


def soap_kernel(
    used_ref, grad_ref, master_ref, first_ref, second_ref, left_ref, right_ref,
    master_out, first_out, second_out,
):
    count = grad_ref.shape[0]
    base = pl.program_id(0) * count

    def product(one, other, dims):
        return lax.dot_general(
            one.astype(jnp.bfloat16),
            other.astype(jnp.bfloat16),
            (dims, ((), ())),
            preferred_element_type=jnp.float32,
        )

    for start in range(0, count, 5):
        group = range(start, min(start + 5, count))
        lefts = [left_ref[number].astype(jnp.bfloat16) for number in group]
        rights = [right_ref[number].astype(jnp.bfloat16) for number in group]
        grads = [
            jnp.where(used_ref[base + number] > 0, grad_ref[number], jnp.bfloat16(0))
            for number in group
        ]
        halves = [product(left, grad, ((0,), (0,))) for left, grad in zip(lefts, grads)]
        turned = [product(half, right, ((1,), (0,))) for half, right in zip(halves, rights)]
        normals = []
        for number, rotated in zip(group, turned):
            first_new = BETA_FIRST * first_ref[number] + (1.0 - BETA_FIRST) * rotated
            second_new = BETA_SECOND * second_ref[number] + (1.0 - BETA_SECOND) * rotated * rotated
            first_out[number] = first_new
            second_out[number] = second_new
            normals.append(first_new / (jnp.sqrt(second_new) + ADAM_EPS))
        halves = [product(left, normal, ((1,), (0,))) for left, normal in zip(lefts, normals)]
        updates = [product(half, right, ((1,), (1,))) for half, right in zip(halves, rights)]
        for number, update in zip(group, updates):
            master = master_ref[number]
            scale = jnp.sqrt(jnp.mean(master * master, keepdims=True) + SCALE_EPS)
            master_out[number] = master - RELATIVE_RATE * scale * (update + WEIGHT_DECAY * master)


def soap_step(used, grads, *state):
    slots = grads.shape[0]
    count = max(number for number in range(1, 11) if slots % number == 0)
    tiles = pl.BlockSpec((count, BLOCK, BLOCK), lambda step, flags: (step, 0, 0))
    whole = jax.ShapeDtypeStruct((slots, BLOCK, BLOCK), jnp.float32)
    return pl.pallas_call(
        soap_kernel,
        out_shape=(whole, whole, whole),
        grid_spec=pltpu.PrefetchScalarGridSpec(
            num_scalar_prefetch=1,
            grid=(slots // count,),
            in_specs=[tiles] * 6,
            out_specs=(tiles, tiles, tiles),
        ),
        compiler_params=pltpu.CompilerParams(
            dimension_semantics=("arbitrary",), vmem_limit_bytes=40 * 1024 * 1024
        ),
    )(used, grads, *state)


def rotate(values, positions, direction):
    half_size = HD // 2
    frequency = ROPE_BASE ** (-2.0 * jnp.arange(half_size, dtype=jnp.float32) / HD)
    angles = positions.astype(jnp.float32)[:, None] * frequency[None, :]
    cosine = jnp.cos(angles)[:, None, :]
    sine = direction * jnp.sin(angles)[:, None, :]
    first_half = values[..., :half_size]
    second_half = values[..., half_size:]
    return jnp.concatenate(
        [first_half * cosine - second_half * sine, second_half * cosine + first_half * sine],
        axis=-1,
    )


def forward_product(left_side, weight):
    return jnp.dot(left_side, weight, preferred_element_type=jnp.float32)


def back_product(grads, weight):
    return jnp.einsum("nf,df->nd", grads, weight, preferred_element_type=jnp.float32)


def outer_product(left_side, right_side):
    return jnp.einsum(
        "nb,nc->bc", left_side, right_side, preferred_element_type=jnp.float32
    ).astype(jnp.bfloat16)


def norm_backward(values, inverse, gain, grad_normed):
    scaled = values * inverse
    gained = grad_normed * gain
    grad_values = inverse * (gained - scaled * jnp.mean(gained * scaled, axis=-1, keepdims=True))
    return (grad_values, jnp.sum(grad_normed * scaled, axis=0))


def local(
    tokens,
    cotangent,
    lengths,
    owner_slot,
    master,
    moment_first,
    moment_second,
    basis_left,
    basis_right,
    small_master,
    small_first,
    small_second,
):
    uly_count = lax.axis_size("uly")
    blk_count = lax.axis_size("blk")
    all_count = lax.axis_size("dp") * blk_count * uly_count
    uly_index = lax.axis_index("uly")
    blk_index = lax.axis_index("blk")
    seq_count = tokens.shape[0]
    rows_local = tokens.shape[1]
    token_count = seq_count * rows_local
    span_rows = rows_local * uly_count
    heads_local = QH // uly_count
    slot_local = master.shape[0]
    slot_total = slot_local * all_count
    score_root = math.sqrt(HD)
    positions = (blk_index * uly_count + uly_index) * rows_local + jnp.arange(
        rows_local, dtype=jnp.int32
    )
    query_pos = blk_index * span_rows + jnp.arange(span_rows, dtype=jnp.int32)
    head_of = [member * heads_local // (QH // KVH) for member in range(uly_count)]
    shard_groups = -(-GRID_FF // (blk_count * STEP_GROUPS)) * STEP_GROUPS
    shard_rows = -(-GRID_D // blk_count)
    attn_cap = capacity(ATTN_TILES / all_count, 3.8, slot_local)
    route = Route(shard_owners(owner_slot, blk_count, shard_groups), slot_local, (3.5, 3.45))
    attn_route = Route(attention_owners(owner_slot, blk_count, shard_rows), slot_local, (5.0, 3.8))
    my_first = route.first
    attn_owner = owner_slot[:ATTN_TILES]
    attn_device = attn_owner // slot_local
    attn_rank = earlier_equal(attn_device)
    fits_attn = jnp.max(attn_rank) < attn_cap
    attn_send = locate(
        jnp.arange(attn_cap, dtype=jnp.int32),
        jnp.where(attn_device == route.device, attn_rank, -1),
        attn_owner - my_first,
    )
    attn_place = attn_device * attn_cap + attn_rank

    master_low = master.astype(jnp.bfloat16)
    small_copies = spread(small_master.astype(jnp.bfloat16), ALL_AXES).reshape(-1)
    attn_gathered = lax.all_gather(pick(master_low, attn_send), ALL_AXES, axis=0, tiled=True)

    def whole_tiles(index):
        return pick(lax.all_gather(master_low, ALL_AXES, axis=0, tiled=True), index)

    attn_tiles = lax.cond(
        fits_attn, lambda: pick(attn_gathered, attn_place), lambda: whole_tiles(attn_owner)
    )
    arrived_tiles = exchange(pick(master_low, route.send_index()), "blk")
    shard_buffer = lax.all_gather(
        pick(arrived_tiles, route.compact_index()), COLUMN_AXES, axis=0, tiled=True
    )
    shard_stack = lax.cond(
        route.fits, lambda: pick(shard_buffer, route.place), lambda: whole_tiles(route.my_owner)
    )
    attn_matrices = []
    first = 0
    for row_count, col_count in matrix_shapes()[:4]:
        tile_count = row_count // BLOCK * (col_count // BLOCK)
        attn_matrices.append(
            tiles_to_matrix(
                attn_tiles[first : first + tile_count], row_count // BLOCK, col_count // BLOCK
            )
        )
        first = first + tile_count
    w_query, w_key, w_value, w_out = attn_matrices
    smalls = [member.astype(jnp.float32) for member in split_small(small_copies)]
    gain_first, gain_second, bias_query, bias_key, bias_value = smalls
    valid_rows = (positions[None, :] < lengths[:, None]).astype(jnp.float32)
    seed_grad = (cotangent.astype(jnp.float32) * valid_rows[:, :, None]).reshape(token_count, D)
    seed_low = seed_grad.astype(jnp.bfloat16)
    seed_line = spread(seed_low, "blk").reshape(blk_count * token_count, D)
    token_rows = tokens.reshape(token_count, D).astype(jnp.float32)
    inverse_first = lax.rsqrt(jnp.mean(token_rows * token_rows, axis=-1, keepdims=True) + NORM_EPS)
    normed = (token_rows * inverse_first * gain_first).astype(jnp.bfloat16)
    query_lin = forward_product(normed, w_query) + bias_query
    key_lin = forward_product(normed, w_key) + bias_key
    value_rows = (
        (forward_product(normed, w_value) + bias_value)
        .astype(jnp.bfloat16)
        .reshape(seq_count, rows_local, KVH, HD)
    )
    query_rot = rotate(query_lin.reshape(seq_count, rows_local, QH, HD), positions, 1.0).astype(
        jnp.bfloat16
    )
    key_rot = rotate(key_lin.reshape(seq_count, rows_local, KVH, HD), positions, 1.0).astype(
        jnp.bfloat16
    )
    query_heads = lax.all_to_all(query_rot, "uly", split_axis=2, concat_axis=1, tiled=True)
    normed_columns = split_columns(normed, blk_count, shard_rows)
    query_heads, seed_line, normed_columns = lax.optimization_barrier(
        (query_heads, seed_line, normed_columns)
    )
    key_value = jnp.concatenate([key_rot, value_rows], axis=-1)
    key_value = jnp.stack([key_value[:, :, head] for head in head_of], axis=0)
    key_value = exchange(key_value, "uly").transpose(1, 0, 2, 3)
    key_value = spread(key_value, "blk").transpose(1, 0, 2, 3, 4)
    key_value = key_value.reshape(seq_count, blk_count * span_rows, 2 * HD)
    keys = key_value[..., :HD]
    values = key_value[..., HD:]
    key_pos = jnp.arange(blk_count * span_rows, dtype=jnp.int32)
    allowed = (key_pos[None, None, :] <= query_pos[None, :, None]) & (
        key_pos[None, None, :] < lengths[:, None, None]
    )
    allowed = allowed[:, :, None, :]
    scores = (
        jnp.einsum("sqhd,skd->sqhk", query_heads, keys, preferred_element_type=jnp.float32)
        / score_root
    )
    scores = jnp.where(allowed, scores, MASK_FILL)
    top = jnp.max(scores, axis=-1, keepdims=True)
    weights = jnp.where(allowed, jnp.exp(scores - top), 0.0)
    probs = weights / jnp.sum(weights, axis=-1, keepdims=True)
    probs_low = probs.astype(jnp.bfloat16)
    attended = jnp.einsum(
        "sqhk,skd->sqhd", probs_low, values, preferred_element_type=jnp.float32
    )
    out_rows = lax.all_to_all(
        attended.astype(jnp.bfloat16), "uly", split_axis=1, concat_axis=2, tiled=True
    ).reshape(token_count, QW)
    middle = token_rows + forward_product(out_rows, w_out)
    inverse_second = lax.rsqrt(jnp.mean(middle * middle, axis=-1, keepdims=True) + NORM_EPS)
    normed_two = (middle * inverse_second * gain_second).astype(jnp.bfloat16)
    normed_line = spread(normed_two, "blk").reshape(blk_count * token_count, D)
    first_group = jnp.full((1,), blk_index * shard_groups, jnp.int32)
    shard_grads, grad_line, mixed_line = mix_lines(
        first_group, normed_line, seed_line, shard_stack
    )
    out_columns = split_columns(out_rows, blk_count, shard_rows)
    grad_line, out_columns = lax.optimization_barrier((grad_line, out_columns))
    grad_normed_two = exchange_sum(grad_line.reshape(blk_count, token_count, D), "blk")
    home_buffer = route.home_buffer(shard_grads)
    grad_normed_two, home_buffer = lax.optimization_barrier((grad_normed_two, home_buffer))
    summed_tiles = route.sum_columns(home_buffer)
    norm_part_two, gain_second_grad = norm_backward(
        middle, inverse_second, gain_second, grad_normed_two
    )
    grad_middle = seed_grad + norm_part_two
    grad_middle_low = grad_middle.astype(jnp.bfloat16)
    grad_out_rows = (
        back_product(grad_middle_low, w_out)
        .astype(jnp.bfloat16)
        .reshape(seq_count, rows_local, QH, HD)
    )
    grad_heads = lax.all_to_all(grad_out_rows, "uly", split_axis=2, concat_axis=1, tiled=True)
    middle_source, grad_heads = lax.optimization_barrier((grad_middle_low, grad_heads))
    middle_lines = spread(middle_source, "blk").reshape(blk_count * token_count, D)
    grad_heads_wide = grad_heads.astype(jnp.float32)
    row_delta = jnp.sum(grad_heads_wide * attended, axis=-1)

    grad_prob = jnp.einsum(
        "sqhd,skd->sqhk", grad_heads, values, preferred_element_type=jnp.float32
    )
    grad_score = (probs * (grad_prob - row_delta[..., None])).astype(jnp.bfloat16)
    grad_query = jnp.einsum(
        "sqhk,skd->sqhd", grad_score, keys, preferred_element_type=jnp.float32
    )
    grad_keys = jnp.einsum(
        "sqhk,sqhd->skd", grad_score, query_heads, preferred_element_type=jnp.float32
    )
    grad_values = jnp.einsum(
        "sqhk,sqhd->skd", probs_low, grad_heads, preferred_element_type=jnp.float32
    )
    grad_query_low = (grad_query / score_root).astype(jnp.bfloat16)
    grad_query_rows = lax.all_to_all(grad_query_low, "uly", split_axis=1, concat_axis=2, tiled=True)
    grad_pair = jnp.concatenate([grad_keys / score_root, grad_values], axis=-1).astype(jnp.bfloat16)
    grad_pair = grad_pair.reshape(seq_count, blk_count, span_rows, 2 * HD).transpose(1, 0, 2, 3)
    grad_pair, middle_lines = lax.optimization_barrier((grad_pair, middle_lines))
    grad_pair = exchange_sum(grad_pair, "blk").astype(jnp.bfloat16)
    grad_pair = grad_pair.reshape(seq_count, uly_count, rows_local, 2 * HD).transpose(1, 0, 2, 3)
    grad_pair = exchange(grad_pair, "uly").astype(jnp.float32)
    grad_pair = jnp.stack(
        [
            sum(grad_pair[member] for member in range(uly_count) if head_of[member] == head)
            for head in range(KVH)
        ],
        axis=2,
    )
    grad_keys_rows = grad_pair[..., :HD]
    grad_values_rows = grad_pair[..., HD:]
    grad_query_lin = (
        rotate(grad_query_rows.astype(jnp.float32), positions, -1.0)
        .astype(jnp.bfloat16)
        .reshape(token_count, QW)
    )
    key_rounded = grad_keys_rows
    grad_key_lin = (
        rotate(key_rounded, positions, -1.0).astype(jnp.bfloat16).reshape(token_count, KVW)
    )
    grad_value_lin = grad_values_rows.astype(jnp.bfloat16).reshape(token_count, KVW)
    grad_normed = (
        back_product(grad_query_lin, w_query)
        + back_product(grad_key_lin, w_key)
        + back_product(grad_value_lin, w_value)
    )
    norm_part_first, gain_first_grad = norm_backward(
        token_rows, inverse_first, gain_first, grad_normed
    )
    grad_tokens = (grad_middle + norm_part_first).reshape(seq_count, rows_local, D)
    small_partial = jnp.concatenate(
        [
            gain_first_grad,
            gain_second_grad,
            jnp.sum(grad_query_lin, axis=0, dtype=jnp.float32),
            jnp.sum(grad_key_lin, axis=0, dtype=jnp.float32),
            jnp.sum(grad_value_lin, axis=0, dtype=jnp.float32),
        ]
    )
    grad_small = exchange_sum(small_partial.reshape(all_count, -1), ALL_AXES)
    grad_lines = spread(
        jnp.concatenate([grad_query_lin, grad_key_lin, grad_value_lin], axis=1), "blk"
    ).reshape(blk_count * token_count, QW + 2 * KVW)
    grad_lines, summed_tiles = lax.optimization_barrier((grad_lines, summed_tiles))
    back_tiles = route.back_buffer(summed_tiles)
    attn_grads = jnp.concatenate(
        [
            matrix_to_tiles(
                outer_product(normed_columns, grad_lines)
            ),
            matrix_to_tiles(
                outer_product(out_columns, middle_lines)
            ),
        ],
        axis=0,
    )
    attn_buffer = attn_route.home_buffer(attn_grads)
    attn_buffer, back_tiles = lax.optimization_barrier((attn_buffer, back_tiles))
    returned_grads = exchange(back_tiles, "blk")
    attn_returned = exchange(attn_route.back_buffer(attn_route.sum_columns(attn_buffer)), "blk")
    my_slots = my_first + jnp.arange(slot_local, dtype=jnp.int32)
    slot_index = locate(my_slots, route.owner, route.slot_position()) + locate(
        my_slots, attn_route.owner, blk_count * route.pair_cap + attn_route.slot_position()
    )
    slot_used = jnp.any(my_slots[:, None] == owner_slot[None, :], axis=1)

    def routed_grads():
        return pick(jnp.concatenate([returned_grads, attn_returned], axis=0), slot_index)

    def summed_grads():
        every_slot = jnp.arange(slot_total, dtype=jnp.int32)
        tile_owner = jnp.concatenate([route.my_owner, attn_route.my_owner])
        index = locate(every_slot, tile_owner, jnp.arange(tile_owner.shape[0], dtype=jnp.int32))
        held = jnp.any(every_slot[:, None] == tile_owner[None, :], axis=1)
        parts = pick(jnp.concatenate([shard_grads, attn_grads], axis=0), index)
        parts = jnp.where(held[:, None, None], parts, 0)
        return lax.psum_scatter(parts, ALL_AXES, scatter_dimension=0, tiled=True)

    grad_slots = lax.cond(route.fits & attn_route.fits, routed_grads, summed_grads)
    grad_slots, mixed_line = lax.optimization_barrier((grad_slots, mixed_line))
    mixed_out = (
        (middle + exchange_sum(mixed_line.reshape(blk_count, token_count, D), "blk"))
        .astype(jnp.bfloat16)
        .reshape(seq_count, rows_local, D)
    )
    master_new, first_new, second_new = soap_step(
        slot_used.astype(jnp.int32),
        grad_slots,
        master,
        moment_first,
        moment_second,
        basis_left,
        basis_right,
    )
    small_first_new = BETA_FIRST * small_first + (1.0 - BETA_FIRST) * grad_small
    small_second_new = BETA_SECOND * small_second + (1.0 - BETA_SECOND) * grad_small * grad_small
    small_new = small_master - SMALL_RATE * (
        small_first_new / (jnp.sqrt(small_second_new) + ADAM_EPS) + WEIGHT_DECAY * small_master
    )
    return (
        mixed_out,
        grad_tokens,
        first_new,
        second_new,
        master_new,
        small_first_new,
        small_second_new,
        small_new,
    )


def solution(mesh):
    in_specs = (
        P("dp", ("blk", "uly"), None),
        P("dp", ("blk", "uly"), None),
        P("dp"),
        P(),
        P(("dp", "blk", "uly"), None, None),
        P(("dp", "blk", "uly"), None, None),
        P(("dp", "blk", "uly"), None, None),
        P(("dp", "blk", "uly"), None, None),
        P(("dp", "blk", "uly"), None, None),
        P(("dp", "blk", "uly")),
        P(("dp", "blk", "uly")),
        P(("dp", "blk", "uly")),
    )
    out_specs = (
        P("dp", ("blk", "uly"), None),
        P("dp", ("blk", "uly"), None),
        P(("dp", "blk", "uly"), None, None),
        P(("dp", "blk", "uly"), None, None),
        P(("dp", "blk", "uly"), None, None),
        P(("dp", "blk", "uly")),
        P(("dp", "blk", "uly")),
        P(("dp", "blk", "uly")),
    )
    return jax.shard_map(local, mesh=mesh, in_specs=in_specs, out_specs=out_specs, check_vma=False)
```
